32 devices in a mesh: dp: 8 (over z, y), tm: 4 (over x, core).
Axes of the slice: x: 2, y: 2, z: 4, core: 2. Of those that a mesh axis runs over, the one named last changes fastest.
Arguments:
- latents: bfloat16 [8, 16, 16, 16, 640], P('dp', 'tm'), may hold values from -60 to 60
- cotangent: bfloat16 [8, 8, 16, 16, 640], P('dp', 'tm'), may hold values from -6 to 6
- timesteps: int32 [8], P('dp'), may hold values from 0 to 999
- spatial_weight: bfloat16 [640, 5760], P('dp'), may hold values from -0.078125 to 0.078125
- temporal_weight: bfloat16 [640, 1920], P('dp'), may hold values from -0.125 to 0.125
- time_weight: bfloat16 [640, 256], P('dp'), may hold values from -0.375 to 0.375
Outputs:
- downsampled: float32 [8, 8, 16, 16, 640], P('dp', 'tm')
- latents_grad: float32 [8, 16, 16, 16, 640], P('dp', 'tm')
- spatial_grad: float32 [640, 5760], P('dp')
- temporal_grad: float32 [640, 1920], P('dp')
- time_grad: float32 [640, 256], P('dp')
The draws below stay inside these ranges and needn't reach their ends.
All inputs are finite; a program needn't handle non-finite values.
Results may differ from the reference program's by a relative error of at most 0.0041.
Values may be sent and summed in bfloat16 or wider, within the bound.
No kernel may reach another device: no remote copies, remote signals or barrier semaphores. Data moves between devices by JAX's collectives and lax.ppermute only.
A program may use at most 128 MiB of HBM per device.

```python
import math
import jax
import jax.numpy as jnp
from jax import lax

C = 640
GROUPS = 32
TE = 256
SIDE = 16
CLIPS = 8
FRAMES = 16
OFRAMES = 8


def draw_latents(key, part):
    key_values, key_channels, key_pixels = jax.random.split(key, 3)
    full_shape = (CLIPS, FRAMES, SIDE, SIDE, C)
    chan_scale = jnp.exp(jax.random.uniform(key_channels, (C,), jnp.float32, math.log(0.3), math.log(3.0)))
    pixel_scale = jnp.exp(jax.random.uniform(key_pixels, (CLIPS, FRAMES, SIDE, SIDE, 1), jnp.float32, math.log(0.5), math.log(5.0)))
    raw_values = jax.random.truncated_normal(key_values, -4.0, 4.0, full_shape, jnp.float32)
    return (raw_values * chan_scale * pixel_scale).astype(jnp.bfloat16)


def set_ends(drawn, rng, least, high):
    extent = drawn.shape
    place = [jax.random.randint(jax.random.fold_in(rng, axis), (), 0, extent[axis]) for axis in range(len(extent))]
    drawn = drawn.at[tuple(place)].set(least)
    longest = extent.index(max(extent))
    place[longest] = (place[longest] + 1) % extent[longest]
    return drawn.at[tuple(place)].set(high)


def steps_of(stream_key, dims, cuts, smallest, largest):
    def one(position, shards_of):
        steps = jax.random.uniform(jax.random.fold_in(jax.random.fold_in(stream_key, 6), position), (shards_of,), jnp.float32, smallest / len(cuts), largest / len(cuts))
        return jnp.repeat(jnp.exp(steps), dims[position] // shards_of).reshape((-1,) + (1,) * (len(dims) - position - 1))

    level = one(*cuts[0])
    for cut in cuts[1:]:
        level = level * one(*cut)
    return level


def scatter_about(own_key, shape, scale, limit, cuts=(), kind=jnp.bfloat16):
    drawn = scale * jax.random.normal(own_key, shape, jnp.float32)
    if cuts:
        drawn = drawn * steps_of(own_key, shape, cuts, -0.22, 0.18)
    return jnp.clip(drawn, -limit, limit).astype(kind)


def setup_inputs(seed: int = 0) -> dict:
    arg_keys = jax.random.split(jax.random.key(seed), 7)
    latents = draw_latents(jax.random.fold_in(arg_keys[6], 71), 0)
    cotangent = scatter_about(arg_keys[1], (CLIPS, OFRAMES, SIDE, SIDE, C), 1.0, 6.0, ((0, 8), (1, 4)))
    timesteps = set_ends(jax.random.randint(arg_keys[2], (CLIPS,), 0, 1000), jax.random.fold_in(arg_keys[2], 1), 0, 999).astype(jnp.int32)
    spatial_weight = scatter_about(arg_keys[3], (C, 9 * C), (9 * C) ** -0.5, 0.078125, ((0, 8),))
    temporal_weight = scatter_about(arg_keys[4], (C, 3 * C), (3 * C) ** -0.5, 0.125, ((0, 8),))
    time_weight = scatter_about(arg_keys[5], (C, TE), TE ** -0.5, 0.375, ((0, 8),))
    return dict(latents=latents, cotangent=cotangent, timesteps=timesteps, spatial_weight=spatial_weight, temporal_weight=temporal_weight, time_weight=time_weight)


epsilon = 1e-05
log_base = math.log(10000.0)

def embedding(diffusion_step, embed_width):
    half_width = embed_width // 2
    frequency = jnp.exp(-log_base * jnp.arange(half_width, dtype=jnp.float32) / half_width)
    angles = diffusion_step.astype(jnp.float32) * frequency
    return jnp.concatenate([jnp.cos(angles), jnp.sin(angles)])

def normalize(frames):
    frame_count, height, breadth, channels = frames.shape
    grouped = frames.astype(jnp.float32).reshape(frame_count, height * breadth, GROUPS, channels // GROUPS)
    center = lax.optimization_barrier(jnp.mean(grouped, axis=(1, 3), keepdims=True))
    deviation = grouped - center
    variance = lax.optimization_barrier(jnp.mean(deviation * deviation, axis=(1, 3), keepdims=True))
    scaled = lax.rsqrt(variance + epsilon)
    return (deviation * scaled, scaled)

def spatial_columns(activation):
    frame_count, height, breadth, channels = activation.shape
    padded = jnp.pad(activation, ((0, 0), (1, 1), (1, 1), (0, 0)))
    shifted_views = [padded[:, row_shift:row_shift + height, col_shift:col_shift + breadth, :] for row_shift in range(3) for col_shift in range(3)]
    return jnp.stack(shifted_views, axis=3).reshape(frame_count * height * breadth, 9, channels)

def spatial_fold(pieces, frame_count, height, breadth):
    channels = pieces.shape[-1]
    layout = pieces.reshape(frame_count, height, breadth, 9, channels)
    total = jnp.zeros((frame_count, height + 2, breadth + 2, channels), jnp.float32)
    for row_shift in range(3):
        for col_shift in range(3):
            placed = jnp.pad(layout[:, :, :, 3 * row_shift + col_shift, :], ((0, 0), (row_shift, 2 - row_shift), (col_shift, 2 - col_shift), (0, 0)))
            total = total + placed
    return total[:, 1:height + 1, 1:breadth + 1, :]

def temporal_columns(extended):
    out_count = (extended.shape[0] - 1) // 2
    taps = [extended[offset:offset + 2 * out_count:2] for offset in range(3)]
    return jnp.stack(taps, axis=2).reshape(out_count * extended.shape[1], 3, extended.shape[2])

def temporal_back(parts, incoming):
    lead_tap = parts[:, :, 0, :]
    mid_tap = parts[:, :, 1, :]
    tail_tap = parts[:, :, 2, :]
    even_frames = jnp.concatenate([lead_tap[1:], incoming[None]], axis=0) + tail_tap
    merged = jnp.stack([mid_tap, even_frames], axis=1)
    return (merged.reshape(2 * parts.shape[0], parts.shape[1], parts.shape[3]), lead_tap[0])

def wide_einsum(form, left, right):
    return jnp.einsum(form, left.astype(jnp.float32), right.astype(jnp.float32), precision=lax.Precision.HIGHEST)

def reference(latents, cotangent, timesteps, spatial_weight, temporal_weight, time_weight):
    channels = latents.shape[-1]
    spatial_taps = spatial_weight.reshape(channels, 9, channels)
    temporal_taps = temporal_weight.reshape(channels, 3, channels)
    time_wide = time_weight.astype(jnp.float32)

    def one_clip(totals, inputs):
        clip_frames, clip_grad, diffusion_step = inputs
        frame_count, height, breadth = (clip_frames.shape[0], clip_frames.shape[1], clip_frames.shape[2])
        pixels = height * breadth
        embedded = embedding(diffusion_step, time_weight.shape[1])
        time_shift = jnp.dot(time_wide, embedded, precision=lax.Precision.HIGHEST)
        normal, scaled = normalize(clip_frames)
        activation = jax.nn.silu(normal).reshape(frame_count, height, breadth, channels).astype(jnp.bfloat16)
        columns = spatial_columns(activation)
        conv_sum = wide_einsum('rkc,ckq->rq', columns, spatial_taps) + time_shift
        hidden = conv_sum.astype(jnp.bfloat16).reshape(frame_count, pixels, channels)
        before = jnp.zeros((1, pixels, channels), jnp.bfloat16)
        extended = jnp.concatenate([before, hidden], axis=0)
        tcols = temporal_columns(extended)
        out_count = frame_count // 2
        result = wide_einsum('rkc,ckq->rq', tcols, temporal_taps)
        result = result.reshape(out_count, height, breadth, channels)
        grad_out = clip_grad.reshape(out_count * pixels, channels)
        parts = wide_einsum('rq,ckq->rkc', grad_out, temporal_taps).reshape(out_count, pixels, 3, channels)
        hidden_grad, leaving = temporal_back(parts, jnp.zeros((pixels, channels), jnp.float32))
        hidden_back = hidden_grad.astype(jnp.bfloat16).reshape(frame_count * pixels, channels)
        shift_grad = lax.optimization_barrier(jnp.sum(hidden_grad, axis=(0, 1)))
        pieces = wide_einsum('rq,ckq->rkc', hidden_back, spatial_taps)
        activation_grad = spatial_fold(pieces, frame_count, height, breadth)
        sigmoid_value = jax.nn.sigmoid(normal)
        derivative = sigmoid_value * (1.0 + normal * (1.0 - sigmoid_value))
        norm_grad = activation_grad.reshape(normal.shape) * derivative
        mean_one = lax.optimization_barrier(jnp.mean(norm_grad, axis=(1, 3), keepdims=True))
        mean_two = lax.optimization_barrier(jnp.mean(norm_grad * normal, axis=(1, 3), keepdims=True))
        input_grad = ((norm_grad - mean_one - normal * mean_two) * scaled).reshape(frame_count, height, breadth, channels)
        spatial_part = wide_einsum('rkc,rq->ckq', columns, hidden_back).reshape(channels, 9 * channels)
        temporal_part = wide_einsum('rkc,rq->ckq', tcols, grad_out).reshape(channels, 3 * channels)
        time_part = shift_grad[:, None] * embedded[None, :]
        term = jnp.concatenate([spatial_part, temporal_part, time_part], axis=1)
        return (totals + term, (result, input_grad))
    initial = jnp.zeros((channels, 12 * channels + time_weight.shape[1]), jnp.float32)
    totals, (downsampled, latents_grad) = lax.scan(one_clip, initial, (latents, cotangent, timesteps))
    spatial_grad = totals[:, :9 * channels]
    temporal_grad = totals[:, 9 * channels:12 * channels]
    time_grad = totals[:, 12 * channels:]
    return (downsampled, latents_grad, spatial_grad, temporal_grad, time_grad)
```

```python
import math

import jax
import jax.numpy as jnp
from jax import lax
from jax.experimental import pallas as pl
from jax.experimental.pallas import tpu as pltpu
from jax.sharding import PartitionSpec as P

GROUPS = 32


epsilon = 1e-05
log_base = math.log(10000.0)
bf16 = jnp.bfloat16
f32 = jnp.float32
VMEM_BYTES = 56 * 1024 * 1024


def embedding(diffusion_step, embed_width):
    half_width = embed_width // 2
    frequency = jnp.exp(-log_base * jnp.arange(half_width, dtype=jnp.float32) / half_width)
    angles = diffusion_step.astype(jnp.float32) * frequency
    return jnp.concatenate([jnp.cos(angles), jnp.sin(angles)])


def normalize(frames):
    frame_count, height, breadth, channels = frames.shape
    grouped = frames.astype(jnp.float32).reshape(
        frame_count, height * breadth, GROUPS, channels // GROUPS
    )
    center = jnp.mean(grouped, axis=(1, 3), keepdims=True)
    deviation = grouped - center
    variance = jnp.mean(deviation * deviation, axis=(1, 3), keepdims=True)
    scaled = lax.rsqrt(variance + epsilon)
    return (deviation * scaled, scaled)


def column_views(frames):
    breadth = frames.shape[2]
    padded = jnp.pad(frames, ((0, 0), (1, 1), (1, 1), (0, 0)))
    return jnp.stack([padded[:, :, s : s + breadth, :] for s in range(3)])


def flip(x, axis, mask):
    count = lax.axis_size(axis)
    return lax.ppermute(x, axis, [(i, i ^ mask) for i in range(count)])


def bits_of(count):
    return [1 << i for i in range(count.bit_length() - 1)]


def after(x, *others):
    return lax.optimization_barrier((x,) + others)[0]


def ordered(mine, other, upper, axis):
    low = jnp.where(upper, other, mine)
    high = jnp.where(upper, mine, other)
    return jnp.concatenate([low, high], axis=axis)


def gather_dp(piece, spots):
    count = lax.axis_size("dp")
    masks = bits_of(count)[::-1]
    index = lax.axis_index("dp")
    x = piece.reshape((1,) * len(masks) + piece.shape)
    arrivals = []
    for spot in spots:
        mask = masks[spot]
        got = flip(x, "dp", mask)
        arrivals.append(got)
        x = ordered(x, got, (index & mask) != 0, spot)
    return x, arrivals


def half_of(length):
    return -(-((length + 1) // 2) // 8) * 8


def split_rows(x, upper, rows_axis):
    length = x.shape[rows_axis]
    half = half_of(length)
    low = lax.slice_in_dim(x, 0, half, axis=rows_axis)
    high = lax.slice_in_dim(x, length - half, length, axis=rows_axis)
    return jnp.where(upper, high, low), jnp.where(upper, low, high)


def reduce_stage(x, kind):
    axis, mask, spot = kind
    upper = (lax.axis_index(axis) & mask) != 0
    if axis == "dp":
        low = lax.slice_in_dim(x, 0, 1, axis=spot)
        high = lax.slice_in_dim(x, 1, 2, axis=spot)
        keep, send = jnp.where(upper, high, low), jnp.where(upper, low, high)
    else:
        keep, send = split_rows(x, upper, x.ndim - 2)
    got = flip(send.astype(bf16), axis, mask)
    return keep + got.astype(f32)


def join_rows(x, length, kind):
    axis, mask, _ = kind
    upper = (lax.axis_index(axis) & mask) != 0
    got = flip(x, axis, mask)
    half = x.shape[0]
    low = jnp.where(upper, got, x)
    high = jnp.where(upper, x, got)
    return jnp.concatenate([low, high[2 * half - length :]], axis=0)


def reduce_all(x, order):
    count = lax.axis_size("dp")
    nbits = len(bits_of(count))
    rows = x.shape[1]
    x = x.reshape((2,) * nbits + x.shape[1:])
    lengths = []
    for kind in order:
        if kind[0] == "tm":
            lengths.append((x.shape[-2], kind))
        x = reduce_stage(x, kind)
    x = x.reshape(x.shape[-2:])
    for length, kind in lengths[::-1]:
        x = join_rows(x, length, kind)
    return x


def matmul_nt(a, b):
    return lax.dot_general(a, b, (((1,), (1,)), ((), ())), preferred_element_type=f32)


def matmul_tn(a, b):
    return lax.dot_general(a, b, (((0,), (0,)), ((), ())), preferred_element_type=f32)


def conv_kernel(back, views_ref, lo_a, hi_a, lo_b, hi_b, mid, shift_ref, out_ref, acc_ref):
    step = pl.program_id(0)
    rows, channels = acc_ref.shape
    height = views_ref.shape[3]

    def part(tap, w):
        r, s = tap // 3, tap % 3
        if back:
            r, s = 2 - r, 2 - s
        x = views_ref[s, :, pl.ds(r, height)].reshape(rows, channels)
        if back:
            return matmul_nt(x, w)
        return jnp.dot(x, w, preferred_element_type=f32)

    @pl.when(step == 0)
    def _():
        acc_ref[...] = part(4, mid[...]) + shift_ref[...]

    acc_ref[...] += part(step, lo_a[...])
    acc_ref[...] += part(5 + step, hi_a[...])
    acc_ref[...] += part(2 + step, lo_b[...])
    acc_ref[...] += part(7 + step, hi_b[...])

    @pl.when(step == 1)
    def _():
        out_ref[...] = acc_ref[...].astype(out_ref.dtype)


def conv(views, taps, shift, back, out_dtype):
    _, frames, _, breadth, channels = views.shape
    rows = frames * (views.shape[2] - 2) * breadth
    w_spec = pl.BlockSpec((channels, channels), lambda i: (0, i))
    return pl.pallas_call(
        lambda *refs: conv_kernel(back, *refs),
        grid=(2,),
        in_specs=[
            pl.BlockSpec(views.shape, lambda i: (0, 0, 0, 0, 0), pipeline_mode=pl.Buffered(1)),
            w_spec,
            w_spec,
            w_spec,
            w_spec,
            pl.BlockSpec((channels, channels), lambda i: (0, 0), pipeline_mode=pl.Buffered(1)),
            pl.BlockSpec((1, channels), lambda i: (0, 0)),
        ],
        out_specs=pl.BlockSpec((rows, channels), lambda i: (0, 0), pipeline_mode=pl.Buffered(1)),
        out_shape=jax.ShapeDtypeStruct((rows, channels), out_dtype),
        scratch_shapes=[pltpu.VMEM((rows, channels), f32)],
        compiler_params=pltpu.CompilerParams(vmem_limit_bytes=VMEM_BYTES),
        name="conv_back" if back else "conv_fwd",
    )(views, *taps, shift)


def hidden_grad_kernel(cot_ref, next_ref, w_ref, back_ref, sum_ref):
    outs = cot_ref.shape[0]
    channels = w_ref.shape[0]
    total = jnp.zeros((1, channels), f32)
    for o in range(outs):
        even = matmul_nt(cot_ref[o], w_ref[:, channels : 2 * channels])
        later = cot_ref[o + 1] if o + 1 < outs else next_ref[...]
        odd = matmul_nt(cot_ref[o], w_ref[:, 2 * channels :]) + matmul_nt(
            later, w_ref[:, :channels]
        )
        back_ref[2 * o] = even.astype(bf16)
        back_ref[2 * o + 1] = odd.astype(bf16)
        total += jnp.sum(even + odd, axis=0, keepdims=True)
    sum_ref[...] = total


def hidden_gradient(cot, following, temporal):
    outs, pixels, channels = cot.shape
    return pl.pallas_call(
        hidden_grad_kernel,
        out_shape=(
            jax.ShapeDtypeStruct((2 * outs, pixels, channels), bf16),
            jax.ShapeDtypeStruct((1, channels), f32),
        ),
        compiler_params=pltpu.CompilerParams(vmem_limit_bytes=VMEM_BYTES),
        name="hidden_grad",
    )(cot, following, temporal)


def weight_grad_kernel(first, views_ref, back_ref, out_ref):
    tap = first + pl.program_id(0)
    rows, channels = back_ref.shape
    height = views_ref.shape[3]
    shards, share, _ = out_ref.shape
    x = views_ref[tap % 3, :, pl.ds(tap // 3, height)].reshape(rows, channels)
    out_ref[...] = matmul_tn(x, back_ref[...]).reshape(shards, share, channels)


def weight_grad(views, hidden_back, first, taps, shards):
    rows, channels = hidden_back.shape
    share = channels // shards
    return pl.pallas_call(
        lambda *refs: weight_grad_kernel(first, *refs),
        grid=(taps,),
        in_specs=[
            pl.BlockSpec(views.shape, lambda i: (0, 0, 0, 0, 0), pipeline_mode=pl.Buffered(1)),
            pl.BlockSpec((rows, channels), lambda i: (0, 0), pipeline_mode=pl.Buffered(1)),
        ],
        out_specs=pl.BlockSpec((shards, share, channels), lambda i: (0, i, 0)),
        out_shape=jax.ShapeDtypeStruct((shards, taps * share, channels), f32),
        compiler_params=pltpu.CompilerParams(vmem_limit_bytes=VMEM_BYTES),
        name="weight_grad",
    )(views, hidden_back)


def body(latents, cotangent, timesteps, spatial_weight, temporal_weight, time_weight):
    clip_frames = latents[0]
    frame_count, height, breadth, channels = clip_frames.shape
    pixels = height * breadth
    out_count = frame_count // 2
    dp = lax.axis_size("dp")
    tm = lax.axis_size("tm")
    share = channels // dp
    dp_masks = bits_of(dp)[::-1]
    nbits = len(dp_masks)
    dp_index = lax.axis_index("dp")
    tm_index = lax.axis_index("tm")
    core = tm_index & 1
    side = (tm_index >> 1) & 1
    on_side = side != 0
    on_core = core != 0

    cot = cotangent[0].reshape(out_count, pixels, channels)
    following = lax.ppermute(cot[0], "tm", [(i + 1, i) for i in range(tm - 1)])

    half = share // 2
    wide = jnp.concatenate([temporal_weight, time_weight], axis=1)
    spots = list(range(nbits))
    piece = lax.dynamic_slice_in_dim(wide, core * half, half, axis=0)
    got, arrivals = gather_dp(piece, spots)
    got = ordered(got, flip(got, "tm", 1), on_core, got.ndim - 2)
    wide_full = got.reshape(channels, wide.shape[1])
    temporal_full = wide_full[:, : 3 * channels]
    time_full = wide_full[:, 3 * channels :]

    my_rows = lax.dynamic_slice_in_dim(spatial_weight, core * half, half, axis=0)
    gate = arrivals[-2]

    def spatial_taps(first, across):
        nonlocal gate
        start = first * channels + (side * 5 * channels if across else 0)
        cols = (2 if across else 1) * channels
        chunk = lax.dynamic_slice_in_dim(my_rows, start, cols, axis=1)
        got, arrivals = gather_dp(after(chunk, gate), spots)
        gate = arrivals[-2]
        if not across:
            whole = ordered(got, flip(got, "tm", 1), on_core, got.ndim - 2)
            return (whole.reshape(channels, cols),)
        other = flip(got, "tm", 2)
        both = jnp.stack([jnp.where(on_side, other, got), jnp.where(on_side, got, other)])
        whole = ordered(both, flip(both, "tm", 1), on_core, both.ndim - 2)
        whole = whole.reshape(2, channels, cols)
        return whole[0], whole[1]

    lo_a, hi_a = spatial_taps(0, True)
    lo_b, hi_b = spatial_taps(2, True)
    (mid,) = spatial_taps(4, False)
    taps = (lo_a, hi_a, lo_b, hi_b, mid)

    normal, scaled = normalize(clip_frames)
    activation = jax.nn.silu(normal).reshape(frame_count, height, breadth, channels).astype(bf16)
    views = column_views(activation)

    hidden_back, shift_sum = hidden_gradient(cot, following, temporal_full)
    flat_back = hidden_back.reshape(frame_count * pixels, channels)

    bit = {"y": ("dp", dp_masks[-1], nbits - 1)}
    z_kinds = [("dp", m, i) for i, m in list(enumerate(dp_masks))[:-1]][::-1]
    y_kinds = [bit["y"]]
    core_kind = [("tm", 1, None)]
    x_kinds = [("tm", m, None) for m in bits_of(tm)[1:]]
    orders = [
        core_kind + y_kinds + z_kinds + x_kinds,
        core_kind + z_kinds + x_kinds + y_kinds,
        core_kind + x_kinds + y_kinds + z_kinds,
    ]
    spatial_rows = []
    for i in range(3):
        grad = weight_grad(views, flat_back, 3 * i, 3, dp)
        total = reduce_all(grad, orders[i])
        spatial_rows.append(total.reshape(3, share, channels))

    embedded = embedding(timesteps[0], time_full.shape[1])
    time_shift = jnp.dot(time_full.astype(f32), embedded, precision=lax.Precision.HIGHEST)
    hidden = conv(views, taps, time_shift[None], False, bf16).reshape(
        frame_count, pixels, channels
    )
    before = lax.ppermute(hidden[-1], "tm", [(i, i + 1) for i in range(tm - 1)])
    evens = hidden[0::2].reshape(out_count * pixels, channels)
    odds = hidden[1::2].reshape(out_count * pixels, channels)
    leads = jnp.concatenate([before[None], hidden[1:-1:2]], axis=0).reshape(
        out_count * pixels, channels
    )
    flat_cot = cot.reshape(out_count * pixels, channels)
    columns = (leads, evens, odds)
    temporal_rows = []
    for k in range(3):
        grad = lax.dot_general(
            columns[k], flat_cot, (((0,), (0,)), ((), ())), preferred_element_type=f32
        )
        temporal_rows.append(reduce_all(grad.reshape(dp, share, channels), orders[k]))
    result = sum(
        jnp.dot(
            columns[k],
            temporal_full[:, k * channels : (k + 1) * channels],
            preferred_element_type=f32,
        )
        for k in range(3)
    )
    downsampled = result.reshape(1, out_count, height, breadth, channels)

    back_views = column_views(flat_back.reshape(frame_count, height, breadth, channels))
    zero_shift = jnp.zeros((1, channels), f32)
    activation_grad = conv(back_views, taps, zero_shift, True, f32)
    sigmoid_value = jax.nn.sigmoid(normal)
    derivative = sigmoid_value * (1.0 + normal * (1.0 - sigmoid_value))
    norm_grad = activation_grad.reshape(normal.shape) * derivative
    mean_one = jnp.mean(norm_grad, axis=(1, 3), keepdims=True)
    mean_two = jnp.mean(norm_grad * normal, axis=(1, 3), keepdims=True)
    input_grad = ((norm_grad - mean_one - normal * mean_two) * scaled).reshape(
        1, frame_count, height, breadth, channels
    )

    sums = shift_sum
    for mask in bits_of(tm):
        sums = sums + flip(sums, "tm", mask)
    pairs = jnp.concatenate([sums, embedded[None]], axis=1)
    for mask in bits_of(dp):
        pairs = jnp.concatenate([pairs, flip(pairs, "dp", mask)], axis=0)
    mine = lax.dynamic_slice_in_dim(pairs[:, :channels], dp_index * share, share, axis=1)
    time_grad = lax.dot_general(
        mine,
        pairs[:, channels:],
        (((0,), (0,)), ((), ())),
        precision=lax.Precision.HIGHEST,
        preferred_element_type=f32,
    )

    spatial_grad = jnp.concatenate(
        [part[i] for part in spatial_rows for i in range(3)], axis=1
    )
    temporal_grad = jnp.concatenate(temporal_rows, axis=1)
    return (downsampled, input_grad, spatial_grad, temporal_grad, time_grad)


def solution(mesh):
    placed = (
        P("dp", "tm", None, None, None),
        P("dp", "tm", None, None, None),
        P("dp"),
        P("dp", None),
        P("dp", None),
        P("dp", None),
    )
    return jax.shard_map(
        body,
        mesh=mesh,
        in_specs=placed,
        out_specs=(
            P("dp", "tm", None, None, None),
            P("dp", "tm", None, None, None),
            P("dp", None),
            P("dp", None),
            P("dp", None),
        ),
        check_vma=False,
    )
```

```python
import math

import jax
import jax.numpy as jnp
from jax import lax
from jax.experimental import pallas as pl
from jax.experimental.pallas import tpu as pltpu
from jax.sharding import Mesh
from jax.sharding import PartitionSpec as P

GROUPS = 32


epsilon = 1e-05
log_base = math.log(10000.0)
bf16 = jnp.bfloat16
f32 = jnp.float32
VMEM_BYTES = 56 * 1024 * 1024


def embedding(diffusion_step, embed_width):
    half_width = embed_width // 2
    frequency = jnp.exp(-log_base * jnp.arange(half_width, dtype=jnp.float32) / half_width)
    angles = diffusion_step.astype(jnp.float32) * frequency
    return jnp.concatenate([jnp.cos(angles), jnp.sin(angles)])


def flip(x, axis, mask=1):
    count = lax.axis_size(axis)
    return lax.ppermute(x, axis, [(i, i ^ mask) for i in range(count)])


def bits_of(count):
    return [1 << i for i in range(count.bit_length() - 1)]


def params():
    return pltpu.CompilerParams(vmem_limit_bytes=VMEM_BYTES)


def whole(shape):
    return pl.BlockSpec(shape, lambda *_: (0,) * len(shape), pipeline_mode=pl.Buffered(1))


def half_of(length):
    return -(-((length + 1) // 2) // 8) * 8


def is_upper(axis, mask):
    return (lax.axis_index(axis) & mask) != 0


def split_rows(x, upper):
    length = x.shape[-2]
    half = half_of(length)
    low = lax.slice_in_dim(x, 0, half, axis=x.ndim - 2)
    high = lax.slice_in_dim(x, length - half, length, axis=x.ndim - 2)
    return jnp.where(upper, high, low), jnp.where(upper, low, high)


def join_rows(x, length, axis, mask):
    upper = is_upper(axis, mask)
    got = flip(x, axis, mask)
    half = x.shape[0]
    low = jnp.where(upper, got, x)
    high = jnp.where(upper, x, got)
    return jnp.concatenate([low, high[2 * half - length :]], axis=0)


def reduce_all(keep, send):
    shards, taps, half, cols = keep.shape
    x = keep + flip(send, "core").astype(f32)
    x = x.reshape(shards, taps * half, cols)
    lengths = []
    for mask in bits_of(lax.axis_size("x")):
        lengths.append((x.shape[-2], mask))
        mine, other = split_rows(x, is_upper("x", mask))
        x = mine + flip(other.astype(bf16), "x", mask).astype(f32)
    x = lax.all_to_all(x.astype(bf16), "dp", 0, 0)
    x = jnp.sum(x.astype(f32), axis=0)
    for length, mask in lengths[::-1]:
        x = join_rows(x, length, "x", mask)
    x = x.reshape(taps, half, cols)
    got = flip(x, "core")
    upper = is_upper("core", 1)
    return jnp.concatenate([jnp.where(upper, got, x), jnp.where(upper, x, got)], axis=1)


def matmul_nt(a, b):
    return lax.dot_general(a, b, (((1,), (1,)), ((), ())), preferred_element_type=f32)


def matmul_tn(a, b):
    return lax.dot_general(a, b, (((0,), (0,)), ((), ())), preferred_element_type=f32)


def matmul(a, b):
    return jnp.dot(a, b, preferred_element_type=f32)


def group_mean(sums, same_ref, count):
    padded = jnp.broadcast_to(sums, (8, sums.shape[1]))
    total = jnp.dot(
        padded, same_ref[...], precision=lax.Precision.HIGHEST, preferred_element_type=f32
    )
    return total[:1] * (1.0 / count)


def write_views(ref, frame, values, breadth):
    pixels, channels = values.shape
    height = pixels // breadth
    column = lax.broadcasted_iota(jnp.int32, (pixels, channels), 0) & (breadth - 1)
    left = jnp.where(column == 0, 0.0, pltpu.roll(values, 1, 0))
    right = jnp.where(column == breadth - 1, 0.0, pltpu.roll(values, pixels - 1, 0))
    edge = jnp.zeros((1, breadth, channels), bf16)
    for s, moved in enumerate((left, values, right)):
        ref[s, frame, 0:1] = edge
        ref[s, frame, 1 : height + 1] = moved.astype(bf16).reshape(height, breadth, channels)
        ref[s, frame, height + 1 : height + 2] = edge


def norm_kernel(count, breadth, x_ref, same_ref, views_ref, mean_ref, scale_ref):
    for frame in range(x_ref.shape[0]):
        x = x_ref[frame].astype(f32)
        center = group_mean(jnp.sum(x, axis=0, keepdims=True), same_ref, count)
        deviation = x - center
        squares = jnp.sum(deviation * deviation, axis=0, keepdims=True)
        scaled = lax.rsqrt(group_mean(squares, same_ref, count) + epsilon)
        normal = deviation * scaled
        mean_ref[frame] = center
        scale_ref[frame] = scaled
        write_views(views_ref, frame, normal / (1.0 + jnp.exp(-normal)), breadth)


def normalize(frames, same, breadth):
    count, pixels, channels = frames.shape
    height = pixels // breadth
    return pl.pallas_call(
        lambda *refs: norm_kernel(pixels * (channels // GROUPS), breadth, *refs),
        out_shape=(
            jax.ShapeDtypeStruct((3, count, height + 2, breadth, channels), bf16),
            jax.ShapeDtypeStruct((count, 1, channels), f32),
            jax.ShapeDtypeStruct((count, 1, channels), f32),
        ),
        compiler_params=params(),
        name="norm",
    )(frames, same)


def turn_kernel(views_ref, out_ref):
    tap = pl.program_id(0)
    _, channels, rows = out_ref.shape
    height = views_ref.shape[2] - 2
    x = views_ref[tap % 3, :, pl.ds(tap // 3, height)].reshape(rows, channels)
    out_ref[0] = x.T


def turned_columns(views):
    _, frames, high, breadth, channels = views.shape
    rows = frames * (high - 2) * breadth
    return pl.pallas_call(
        turn_kernel,
        grid=(9,),
        in_specs=[whole(views.shape)],
        out_specs=pl.BlockSpec((1, channels, rows), lambda i: (i, 0, 0)),
        out_shape=jax.ShapeDtypeStruct((9, channels, rows), bf16),
        compiler_params=params(),
        name="turn",
    )(views)


def hidden_grad_kernel(breadth, cot_ref, next_ref, w_ref, back_ref, views_ref, sum_ref):
    outs = cot_ref.shape[0]
    channels = w_ref.shape[0]
    total = jnp.zeros((1, channels), f32)
    for o in range(outs):
        later = cot_ref[o + 1] if o + 1 < outs else next_ref[...]
        even = matmul_nt(cot_ref[o], w_ref[:, channels : 2 * channels])
        odd = matmul_nt(cot_ref[o], w_ref[:, 2 * channels : 3 * channels]) + matmul_nt(
            later, w_ref[:, :channels]
        )
        for frame, values in ((2 * o, even), (2 * o + 1, odd)):
            back_ref[frame] = values.astype(bf16)
            write_views(views_ref, frame, values, breadth)
            total += jnp.sum(values, axis=0, keepdims=True)
    sum_ref[...] = total


def hidden_gradient(cot, following, temporal, breadth):
    outs, pixels, channels = cot.shape
    return pl.pallas_call(
        lambda *refs: hidden_grad_kernel(breadth, *refs),
        out_shape=(
            jax.ShapeDtypeStruct((2 * outs, pixels, channels), bf16),
            jax.ShapeDtypeStruct((3, 2 * outs, pixels // breadth + 2, breadth, channels), bf16),
            jax.ShapeDtypeStruct((1, channels), f32),
        ),
        compiler_params=params(),
        name="hidden_grad",
    )(cot, following, temporal)


def store_halves(core_ref, grad, keep_ref, send_ref, slot):
    shards, _, half, channels = keep_ref.shape
    grad = grad.reshape(shards, 2 * half, channels)
    low, high = grad[:, :half], grad[:, half:]

    @pl.when(core_ref[0] == 0)
    def _():
        keep_ref[:, slot] = low
        send_ref[:, slot] = high.astype(bf16)

    @pl.when(core_ref[0] != 0)
    def _():
        keep_ref[:, slot] = high
        send_ref[:, slot] = low.astype(bf16)


def weight_grad_kernel(core_ref, x_ref, back_ref, keep_ref, send_ref):
    store_halves(core_ref, matmul(x_ref[0], back_ref[...]), keep_ref, send_ref, 0)


def weight_grad(turned, hidden_back, shards, core):
    taps = turned.shape[0]
    rows, channels = hidden_back.shape
    half = channels // shards // 2
    out_spec = pl.BlockSpec((shards, 1, half, channels), lambda i: (0, i, 0, 0))
    return pl.pallas_call(
        weight_grad_kernel,
        grid=(taps,),
        in_specs=[
            pl.BlockSpec(memory_space=pltpu.SMEM),
            pl.BlockSpec((1, channels, rows), lambda i: (i, 0, 0)),
            whole((rows, channels)),
        ],
        out_specs=(out_spec, out_spec),
        out_shape=(
            jax.ShapeDtypeStruct((shards, taps, half, channels), f32),
            jax.ShapeDtypeStruct((shards, taps, half, channels), bf16),
        ),
        compiler_params=params(),
        name="weight_grad",
    )(core, turned, hidden_back)


def temporal_grad_kernel(core_ref, hidden_ref, before_ref, cot_ref, keep_ref, send_ref):
    for k in range(3):
        grad = 0.0
        for o in range(cot_ref.shape[0]):
            frame = 2 * o + k - 1
            x = before_ref[...] if frame < 0 else hidden_ref[frame]
            grad += matmul_tn(x, cot_ref[o])
        store_halves(core_ref, grad, keep_ref, send_ref, k)


def temporal_grad_parts(hidden, before, cot, shards, core):
    channels = cot.shape[2]
    half = channels // shards // 2
    vmem = pl.BlockSpec(memory_space=pltpu.VMEM)
    return pl.pallas_call(
        temporal_grad_kernel,
        in_specs=[pl.BlockSpec(memory_space=pltpu.SMEM), vmem, vmem, vmem],
        out_shape=(
            jax.ShapeDtypeStruct((shards, 3, half, channels), f32),
            jax.ShapeDtypeStruct((shards, 3, half, channels), bf16),
        ),
        compiler_params=params(),
        name="temporal_grad",
    )(core, hidden, before, cot)


def temporal_kernel(hidden_ref, before_ref, w_ref, out_ref):
    channels = w_ref.shape[0]
    for o in range(out_ref.shape[0]):
        total = 0.0
        for k in range(3):
            frame = 2 * o + k - 1
            x = before_ref[...] if frame < 0 else hidden_ref[frame]
            total += matmul(x, w_ref[:, k * channels : (k + 1) * channels])
        out_ref[o] = total


def temporal_forward(hidden, before, temporal):
    frames, pixels, channels = hidden.shape
    return pl.pallas_call(
        temporal_kernel,
        out_shape=jax.ShapeDtypeStruct((frames // 2, pixels, channels), f32),
        compiler_params=params(),
        name="temporal",
    )(hidden, before, temporal)


def conv_forward_kernel(views_ref, w_ref, shift_ref, out_ref, acc_ref):
    tap = pl.program_id(0)
    rows, channels = acc_ref.shape
    height = views_ref.shape[2] - 2
    x = views_ref[tap % 3, :, pl.ds(tap // 3, height)].reshape(rows, channels)

    @pl.when(tap == 0)
    def _():
        acc_ref[...] = jnp.broadcast_to(shift_ref[...], (rows, channels))

    acc_ref[...] += matmul(x, w_ref[...])

    @pl.when(tap == 8)
    def _():
        out_ref[...] = acc_ref[...].astype(bf16).reshape(out_ref.shape)


def conv_forward(views, spatial, shift):
    _, frames, high, breadth, channels = views.shape
    pixels = (high - 2) * breadth
    return pl.pallas_call(
        conv_forward_kernel,
        grid=(9,),
        in_specs=[
            whole(views.shape),
            pl.BlockSpec((channels, channels), lambda i: (0, i)),
            whole((1, channels)),
        ],
        out_specs=whole((frames, pixels, channels)),
        out_shape=jax.ShapeDtypeStruct((frames, pixels, channels), bf16),
        scratch_shapes=[pltpu.VMEM((frames * pixels, channels), f32)],
        compiler_params=params(),
        name="conv_forward",
    )(views, spatial, shift)


def conv_back_kernel(
    count, views_ref, w_ref, x_ref, mean_ref, scale_ref, same_ref, out_ref, acc_ref
):
    tap = pl.program_id(0)
    rows, channels = acc_ref.shape
    height = views_ref.shape[2] - 2
    x = views_ref[2 - tap % 3, :, pl.ds(2 - tap // 3, height)].reshape(rows, channels)

    @pl.when(tap == 0)
    def _():
        acc_ref[...] = matmul_nt(x, w_ref[...])

    @pl.when(tap != 0)
    def _():
        acc_ref[...] += matmul_nt(x, w_ref[...])

    @pl.when(tap == 8)
    def _():
        frames, pixels, _ = x_ref.shape
        for frame in range(frames):
            scaled = scale_ref[frame]
            normal = (x_ref[frame].astype(f32) - mean_ref[frame]) * scaled
            gate = 1.0 / (1.0 + jnp.exp(-normal))
            slope = gate * (1.0 + normal * (1.0 - gate))
            grad = acc_ref[frame * pixels : (frame + 1) * pixels] * slope
            one = group_mean(jnp.sum(grad, axis=0, keepdims=True), same_ref, count)
            two = group_mean(jnp.sum(grad * normal, axis=0, keepdims=True), same_ref, count)
            out_ref[frame] = (grad - one - normal * two) * scaled


def conv_back(views, spatial, frames, mean, scale, same):
    count, pixels, channels = frames.shape
    return pl.pallas_call(
        lambda *refs: conv_back_kernel(pixels * (channels // GROUPS), *refs),
        grid=(9,),
        in_specs=[
            whole(views.shape),
            pl.BlockSpec((channels, channels), lambda i: (0, i)),
            whole(frames.shape),
            whole(mean.shape),
            whole(scale.shape),
            whole(same.shape),
        ],
        out_specs=whole(frames.shape),
        out_shape=jax.ShapeDtypeStruct(frames.shape, f32),
        scratch_shapes=[pltpu.VMEM((count * pixels, channels), f32)],
        compiler_params=params(),
        name="conv_back",
    )(views, spatial, frames, mean, scale, same)


def neighbours(x_size, step):
    count = 2 * x_size
    return [(i, i + step) for i in range(count) if 0 <= i + step < count]


def body(latents, cotangent, timesteps, spatial_weight, temporal_weight, time_weight):
    clip_frames = latents[0]
    frame_count, height, breadth, channels = clip_frames.shape
    pixels = height * breadth
    out_count = frame_count // 2
    dp = lax.axis_size("dp")
    x_size = lax.axis_size("x")
    share = channels // dp
    half = share // 2
    core = lax.axis_index("core")
    core_scalar = core[None].astype(jnp.int32)
    frames = clip_frames.reshape(frame_count, pixels, channels)

    cot = cotangent[0].reshape(out_count, pixels, channels)
    following = lax.ppermute(cot[0], ("x", "core"), neighbours(x_size, -1))

    wide = jnp.concatenate([temporal_weight, time_weight], axis=1)
    wide_mine = lax.dynamic_slice_in_dim(wide, core * half, half, axis=0)
    wide_full = lax.all_gather(wide_mine, ("dp", "core"), axis=0, tiled=True)
    spatial_mine = lax.dynamic_slice_in_dim(spatial_weight, core * half, half, axis=0)
    spatial_full = lax.all_gather(spatial_mine, ("dp", "core"), axis=0, tiled=True)

    group = lax.broadcasted_iota(jnp.int32, (channels, channels), 0) // (channels // GROUPS)
    same = (group == group.T).astype(f32)
    views, mean, scale = normalize(frames, same, breadth)
    turned = turned_columns(views)

    hidden_back, back_views, shift_sum = hidden_gradient(cot, following, wide_full, breadth)
    flat_back = hidden_back.reshape(frame_count * pixels, channels)
    spatial_rows = reduce_all(*weight_grad(turned, flat_back, dp, core_scalar))

    time_full = wide_full[:, 3 * channels :]
    embedded = embedding(timesteps[0], time_full.shape[1])
    time_shift = jnp.dot(time_full.astype(f32), embedded, precision=lax.Precision.HIGHEST)
    hidden = conv_forward(views, spatial_full, time_shift[None])
    before = lax.ppermute(hidden[-1], ("x", "core"), neighbours(x_size, 1))
    temporal_rows = reduce_all(*temporal_grad_parts(hidden, before, cot, dp, core_scalar))
    result = temporal_forward(hidden, before, wide_full)
    downsampled = result.reshape(1, out_count, height, breadth, channels)

    input_grad = conv_back(back_views, spatial_full, frames, mean, scale, same)
    input_grad = input_grad.reshape(1, frame_count, height, breadth, channels)

    sums = shift_sum + flip(shift_sum, "core")
    for mask in bits_of(x_size):
        sums = sums + flip(sums, "x", mask)
    pairs = jnp.concatenate([sums, embedded[None]], axis=1)
    for mask in bits_of(dp):
        pairs = jnp.concatenate([pairs, flip(pairs, "dp", mask)], axis=0)
    mine = lax.dynamic_slice_in_dim(
        pairs[:, :channels], lax.axis_index("dp") * share, share, axis=1
    )
    time_grad = lax.dot_general(
        mine,
        pairs[:, channels:],
        (((0,), (0,)), ((), ())),
        precision=lax.Precision.HIGHEST,
        preferred_element_type=f32,
    )

    spatial_grad = jnp.concatenate([spatial_rows[i] for i in range(9)], axis=1)
    temporal_grad = jnp.concatenate([temporal_rows[i] for i in range(3)], axis=1)
    return (downsampled, input_grad, spatial_grad, temporal_grad, time_grad)


def solution(mesh):
    dp, tm = mesh.devices.shape
    fine = Mesh(mesh.devices.reshape(dp, tm // 2, 2), ("dp", "x", "core"))
    placed = (
        P("dp", ("x", "core"), None, None, None),
        P("dp", ("x", "core"), None, None, None),
        P("dp"),
        P("dp", None),
        P("dp", None),
        P("dp", None),
    )
    return jax.shard_map(
        body,
        mesh=fine,
        in_specs=placed,
        out_specs=(
            P("dp", ("x", "core"), None, None, None),
            P("dp", ("x", "core"), None, None, None),
            P("dp", None),
            P("dp", None),
            P("dp", None),
        ),
        check_vma=False,
    )
```

```python
import math

import jax
import jax.numpy as jnp
from jax import lax
from jax.experimental import pallas as pl
from jax.experimental.pallas import tpu as pltpu
from jax.sharding import Mesh
from jax.sharding import PartitionSpec as P

GROUPS = 32


epsilon = 1e-05
log_base = math.log(10000.0)
bf16 = jnp.bfloat16
f32 = jnp.float32
VMEM_BYTES = 56 * 1024 * 1024


def embedding(diffusion_step, embed_width):
    half_width = embed_width // 2
    frequency = jnp.exp(-log_base * jnp.arange(half_width, dtype=jnp.float32) / half_width)
    angles = diffusion_step.astype(jnp.float32) * frequency
    return jnp.concatenate([jnp.cos(angles), jnp.sin(angles)])


def flip(x, axis, mask=1):
    count = lax.axis_size(axis)
    return lax.ppermute(x, axis, [(i, i ^ mask) for i in range(count)])


def bits_of(count):
    return [1 << i for i in range(count.bit_length() - 1)]


def params():
    return pltpu.CompilerParams(vmem_limit_bytes=VMEM_BYTES)


def whole(shape):
    return pl.BlockSpec(shape, lambda *_: (0,) * len(shape), pipeline_mode=pl.Buffered(1))


def is_upper(axis, mask):
    return (lax.axis_index(axis) & mask) != 0


def after(x, *others):
    return lax.optimization_barrier((x,) + others)[0]


def ordered(mine, other, upper, axis):
    low = jnp.where(upper, other, mine)
    high = jnp.where(upper, mine, other)
    return jnp.concatenate([low, high], axis=axis)


def gather_temporal(weight, fillers):
    share, wide = weight.shape
    channels = wide // 3
    half = share // 2
    side = lax.axis_index("x") & 1
    x = lax.dynamic_slice(
        weight, (lax.axis_index("core") * half, side * channels), (half, 2 * channels)
    )
    masks = bits_of(lax.axis_size("dp"))[::-1]
    x = x.reshape((1,) * len(masks) + x.shape)
    for spot, mask in enumerate(masks):
        got = flip(x, "dp", mask)
        if mask == 1:
            got = after(got, fillers[0](x))
        x = ordered(x, got, is_upper("dp", mask), spot)
    upper = side != 0
    low, high = x[..., :channels], x[..., channels:]
    outer = jnp.where(upper, high, low)
    other = after(flip(outer, "x", 1), fillers[1](outer))
    x = jnp.concatenate(
        [jnp.where(upper, other, low), jnp.where(upper, low, high), jnp.where(upper, high, other)],
        axis=-1,
    )
    x = ordered(x, flip(x, "core"), is_upper("core", 1), x.ndim - 2)
    return x.reshape(share * lax.axis_size("dp"), wide)


class Chain:
    def __init__(self, keep, send):
        shards, taps, half, cols = keep.shape
        dp_masks = bits_of(shards)[::-1]
        x_masks = bits_of(lax.axis_size("x"))[::-1]
        nd, nx = len(dp_masks), len(x_masks)
        shape = (2,) * (nd + nx) + (taps >> nx, half, cols)
        self.got = flip(send, "core").reshape(shape)
        self.keep = keep.reshape(shape)
        self.stages = [("x", m, nd + i) for i, m in list(enumerate(x_masks))[::-1]]
        self.stages += [("dp", m, i) for i, m in list(enumerate(dp_masks))[::-1]]

    def launch(self):
        axis, mask, spot = self.stages.pop(0)
        bit = is_upper(axis, mask).astype(jnp.int32)

        def pick(which):
            kept = lax.dynamic_index_in_dim(self.keep, which, spot)
            return kept + lax.dynamic_index_in_dim(self.got, which, spot).astype(f32)

        other = pick(1 - bit).astype(bf16)
        self.keep, self.got = pick(bit), flip(other, axis, mask)
        return other

    def land(self, token):
        self.keep, self.got = lax.optimization_barrier((self.keep, self.got, token))[:2]

    def finish(self):
        while self.stages:
            self.launch()
        x = self.keep + self.got.astype(f32)
        return x.reshape(x.shape[-3:])


def join_x(x, token=None):
    for mask in bits_of(lax.axis_size("x")):
        got = flip(x, "x", mask)
        if token is not None:
            x, got = lax.optimization_barrier((x, got, token))[:2]
        x = ordered(x, got, is_upper("x", mask), 1)
    return x


def join_core(x):
    return ordered(x, flip(x, "core"), is_upper("core", 1), 2)


def matmul_nt(a, b):
    return lax.dot_general(a, b, (((1,), (1,)), ((), ())), preferred_element_type=f32)


def matmul_tn(a, b):
    return lax.dot_general(a, b, (((0,), (0,)), ((), ())), preferred_element_type=f32)


def matmul(a, b):
    return jnp.dot(a, b, preferred_element_type=f32)


def group_mean(sums, same_ref, count):
    filled = -(-len(sums) // 8) * 8
    padded = jnp.concatenate(sums + [sums[0]] * (filled - len(sums)), axis=0)
    total = jnp.dot(
        padded, same_ref[...], precision=lax.Precision.HIGHEST, preferred_element_type=f32
    )
    return total * (1.0 / count)


def write_views(ref, frame, values, breadth):
    pixels, channels = values.shape
    height = pixels // breadth
    column = lax.broadcasted_iota(jnp.int32, (pixels, channels), 0) & (breadth - 1)
    left = jnp.where(column == 0, 0.0, pltpu.roll(values, 1, 0))
    right = jnp.where(column == breadth - 1, 0.0, pltpu.roll(values, pixels - 1, 0))
    edge = jnp.zeros((1, breadth, 3 * channels), bf16)
    ref[frame, 0:1] = edge
    ref[frame, height + 1 : height + 2] = edge
    for s, moved in enumerate((left, values, right)):
        ref[frame, 1 : height + 1, :, s * channels : (s + 1) * channels] = moved.astype(
            bf16
        ).reshape(height, breadth, channels)


def rows_of(views_ref, r):
    frames, high, breadth, wide = views_ref.shape
    return views_ref[:, pl.ds(r, high - 2)].reshape(frames * (high - 2) * breadth, wide)


def norm_kernel(count, breadth, x_ref, same_ref, views_ref, mean_ref, scale_ref):
    frames = range(x_ref.shape[0])
    sums = [jnp.sum(x_ref[f].astype(f32), axis=0, keepdims=True) for f in frames]
    centers = group_mean(sums, same_ref, count)
    squares = []
    for f in frames:
        deviation = x_ref[f].astype(f32) - centers[f : f + 1]
        squares.append(jnp.sum(deviation * deviation, axis=0, keepdims=True))
    scales = lax.rsqrt(group_mean(squares, same_ref, count) + epsilon)
    for f in frames:
        center, scaled = centers[f : f + 1], scales[f : f + 1]
        normal = (x_ref[f].astype(f32) - center) * scaled
        mean_ref[f] = center
        scale_ref[f] = scaled
        write_views(views_ref, f, normal / (1.0 + jnp.exp(-normal)), breadth)


def normalize(frames, same, breadth):
    count, pixels, channels = frames.shape
    height = pixels // breadth
    return pl.pallas_call(
        lambda *refs: norm_kernel(pixels * (channels // GROUPS), breadth, *refs),
        out_shape=(
            jax.ShapeDtypeStruct((count, height + 2, breadth, 3 * channels), bf16),
            jax.ShapeDtypeStruct((count, 1, channels), f32),
            jax.ShapeDtypeStruct((count, 1, channels), f32),
        ),
        compiler_params=params(),
        name="norm",
    )(frames, same)


def turn_kernel(views_ref, out_ref):
    out_ref[0] = rows_of(views_ref, pl.program_id(0)).T


def turned_columns(views):
    frames, high, breadth, wide = views.shape
    rows = frames * (high - 2) * breadth
    return pl.pallas_call(
        turn_kernel,
        grid=(3,),
        in_specs=[whole(views.shape)],
        out_specs=pl.BlockSpec((1, wide, rows), lambda i: (i, 0, 0)),
        out_shape=jax.ShapeDtypeStruct((3, wide, rows), bf16),
        compiler_params=params(),
        name="turn",
    )(views)


def hidden_grad_kernel(breadth, cot_ref, next_ref, w_ref, back_ref, views_ref, sum_ref):
    outs = cot_ref.shape[0]
    channels = w_ref.shape[0]
    total = jnp.zeros((1, channels), f32)
    for o in range(outs):
        later = cot_ref[o + 1] if o + 1 < outs else next_ref[...]
        even = matmul_nt(cot_ref[o], w_ref[:, channels : 2 * channels])
        odd = matmul_nt(cot_ref[o], w_ref[:, 2 * channels : 3 * channels]) + matmul_nt(
            later, w_ref[:, :channels]
        )
        for frame, values in ((2 * o, even), (2 * o + 1, odd)):
            back_ref[frame] = values.astype(bf16)
            write_views(views_ref, frame, values, breadth)
            total += jnp.sum(values, axis=0, keepdims=True)
    sum_ref[...] = total


def hidden_gradient(cot, following, temporal, breadth):
    outs, pixels, channels = cot.shape
    return pl.pallas_call(
        lambda *refs: hidden_grad_kernel(breadth, *refs),
        out_shape=(
            jax.ShapeDtypeStruct((2 * outs, pixels, channels), bf16),
            jax.ShapeDtypeStruct((2 * outs, pixels // breadth + 2, breadth, 3 * channels), bf16),
            jax.ShapeDtypeStruct((1, channels), f32),
        ),
        compiler_params=params(),
        name="hidden_grad",
    )(cot, following, temporal)


def store_halves(core_ref, grad, keep_ref, send_ref, slot):
    shards, _, half, channels = keep_ref.shape
    grad = grad.reshape(shards, 2 * half, channels)
    low, high = grad[:, :half], grad[:, half:]

    @pl.when(core_ref[0] == 0)
    def _():
        keep_ref[:, slot] = low
        send_ref[:, slot] = high.astype(bf16)

    @pl.when(core_ref[0] != 0)
    def _():
        keep_ref[:, slot] = high
        send_ref[:, slot] = low.astype(bf16)


def weight_grad_kernel(core_ref, x_ref, back_ref, keep_ref, send_ref):
    store_halves(core_ref, matmul(x_ref[0], back_ref[...]), keep_ref, send_ref, 0)


def weight_grad(turned, hidden_back, first, shards, core):
    rows, channels = hidden_back.shape
    half = channels // shards // 2
    out_spec = pl.BlockSpec((shards, 1, half, channels), lambda i: (0, i, 0, 0))
    return pl.pallas_call(
        weight_grad_kernel,
        grid=(4,),
        in_specs=[
            pl.BlockSpec(memory_space=pltpu.SMEM),
            pl.BlockSpec((1, channels, rows), lambda i: (first + i, 0, 0)),
            whole((rows, channels)),
        ],
        out_specs=(out_spec, out_spec),
        out_shape=(
            jax.ShapeDtypeStruct((shards, 4, half, channels), f32),
            jax.ShapeDtypeStruct((shards, 4, half, channels), bf16),
        ),
        compiler_params=params(),
        name="weight_grad",
    )(core, turned, hidden_back)


def last_grad_kernel(
    core_ref, x_ref, back_ref, hidden_ref, before_ref, cot_ref, keep_ref, send_ref
):
    store_halves(core_ref, matmul(x_ref[0], back_ref[...]), keep_ref, send_ref, 0)
    for k in range(3):
        grad = 0.0
        for o in range(cot_ref.shape[0]):
            frame = 2 * o + k - 1
            x = before_ref[...] if frame < 0 else hidden_ref[frame]
            grad += matmul_tn(x, cot_ref[o])
        store_halves(core_ref, grad, keep_ref, send_ref, 1 + k)


def last_grad(turned, hidden_back, hidden, before, cot, shards, core):
    rows, channels = hidden_back.shape
    half = channels // shards // 2
    shape = (shards, 4, half, channels)
    return pl.pallas_call(
        last_grad_kernel,
        grid=(1,),
        in_specs=[
            pl.BlockSpec(memory_space=pltpu.SMEM),
            pl.BlockSpec((1, channels, rows), lambda i: (8, 0, 0)),
            whole((rows, channels)),
            whole(hidden.shape),
            whole(before.shape),
            whole(cot.shape),
        ],
        out_specs=(whole(shape), whole(shape)),
        out_shape=(jax.ShapeDtypeStruct(shape, f32), jax.ShapeDtypeStruct(shape, bf16)),
        compiler_params=params(),
        name="last_grad",
    )(core, turned, hidden_back, hidden, before, cot)


def temporal_kernel(hidden_ref, before_ref, w_ref, out_ref):
    channels = w_ref.shape[0]
    for o in range(out_ref.shape[0]):
        total = 0.0
        for k in range(3):
            frame = 2 * o + k - 1
            x = before_ref[...] if frame < 0 else hidden_ref[frame]
            total += matmul(x, w_ref[:, k * channels : (k + 1) * channels])
        out_ref[o] = total


def temporal_forward(hidden, before, temporal):
    frames, pixels, channels = hidden.shape
    return pl.pallas_call(
        temporal_kernel,
        out_shape=jax.ShapeDtypeStruct((frames // 2, pixels, channels), f32),
        compiler_params=params(),
        name="temporal",
    )(hidden, before, temporal)


def conv_forward_kernel(views_ref, w_ref, shift_ref, out_ref, acc_ref, tall_ref):
    r = pl.program_id(0)
    rows, channels = acc_ref.shape
    for s in range(3):
        tall_ref[s * channels : (s + 1) * channels] = w_ref[:, s * channels : (s + 1) * channels]
    part = matmul(rows_of(views_ref, r), tall_ref[...])

    @pl.when(r == 0)
    def _():
        acc_ref[...] = part + shift_ref[...]

    @pl.when(r == 1)
    def _():
        acc_ref[...] += part

    @pl.when(r == 2)
    def _():
        out_ref[...] = (acc_ref[...] + part).astype(bf16).reshape(out_ref.shape)


def conv_forward(views, spatial, shift):
    frames, high, breadth, wide = views.shape
    channels = wide // 3
    pixels = (high - 2) * breadth
    return pl.pallas_call(
        conv_forward_kernel,
        grid=(3,),
        in_specs=[
            whole(views.shape),
            pl.BlockSpec((channels, wide), lambda i: (0, i)),
            whole((1, channels)),
        ],
        out_specs=whole((frames, pixels, channels)),
        out_shape=jax.ShapeDtypeStruct((frames, pixels, channels), bf16),
        scratch_shapes=[
            pltpu.VMEM((frames * pixels, channels), f32),
            pltpu.VMEM((wide, channels), bf16),
        ],
        compiler_params=params(),
        name="conv_forward",
    )(views, spatial, shift)


def back_part(views_ref, w_ref, r):
    channels = w_ref.shape[0]
    x = rows_of(views_ref, 2 - r)
    x = jnp.concatenate(
        [x[:, (2 - s) * channels : (3 - s) * channels] for s in range(3)], axis=1
    )
    return matmul_nt(x, w_ref[...])


def conv_back_kernel(views_ref, w_ref, acc_ref):
    r = pl.program_id(0)
    part = back_part(views_ref, w_ref, r)

    @pl.when(r == 0)
    def _():
        acc_ref[...] = part

    @pl.when(r != 0)
    def _():
        acc_ref[...] += part


def conv_back_start(views, spatial):
    frames, high, breadth, wide = views.shape
    channels = wide // 3
    rows = frames * (high - 2) * breadth
    return pl.pallas_call(
        conv_back_kernel,
        grid=(2,),
        in_specs=[whole(views.shape), pl.BlockSpec((channels, wide), lambda i: (0, i))],
        out_specs=whole((rows, channels)),
        out_shape=jax.ShapeDtypeStruct((rows, channels), f32),
        compiler_params=params(),
        name="conv_back_start",
    )(views, spatial)


def conv_back_end_kernel(
    count, views_ref, w_ref, part_ref, x_ref, mean_ref, scale_ref, same_ref, out_ref, acc_ref
):
    acc_ref[...] = part_ref[...] + back_part(views_ref, w_ref, 2)
    frames, pixels, _ = x_ref.shape

    def parts(f):
        normal = (x_ref[f].astype(f32) - mean_ref[f]) * scale_ref[f]
        gate = 1.0 / (1.0 + jnp.exp(-normal))
        slope = gate * (1.0 + normal * (1.0 - gate))
        return normal, slope

    sums = []
    for f in range(frames):
        normal, slope = parts(f)
        grad = acc_ref[f * pixels : (f + 1) * pixels] * slope
        acc_ref[f * pixels : (f + 1) * pixels] = grad
        sums.append(jnp.sum(grad, axis=0, keepdims=True))
        sums.append(jnp.sum(grad * normal, axis=0, keepdims=True))
    means = group_mean(sums, same_ref, count)
    for f in range(frames):
        normal = (x_ref[f].astype(f32) - mean_ref[f]) * scale_ref[f]
        one, two = means[2 * f : 2 * f + 1], means[2 * f + 1 : 2 * f + 2]
        grad = acc_ref[f * pixels : (f + 1) * pixels]
        out_ref[f] = (grad - one - normal * two) * scale_ref[f]


def conv_back_end(views, spatial, part, frames, mean, scale, same):
    count, pixels, channels = frames.shape
    return pl.pallas_call(
        lambda *refs: conv_back_end_kernel(pixels * (channels // GROUPS), *refs),
        grid=(1,),
        in_specs=[
            whole(views.shape),
            pl.BlockSpec((channels, 3 * channels), lambda i: (0, 2)),
            whole(part.shape),
            whole(frames.shape),
            whole(mean.shape),
            whole(scale.shape),
            whole(same.shape),
        ],
        out_specs=whole(frames.shape),
        out_shape=jax.ShapeDtypeStruct(frames.shape, f32),
        scratch_shapes=[pltpu.VMEM((count * pixels, channels), f32)],
        compiler_params=params(),
        name="conv_back_end",
    )(views, spatial, part, frames, mean, scale, same)


def neighbours(x_size, step):
    count = 2 * x_size
    return [(i, i + step) for i in range(count) if 0 <= i + step < count]


def body(latents, cotangent, timesteps, spatial_weight, temporal_weight, time_weight):
    clip_frames = latents[0]
    frame_count, height, breadth, channels = clip_frames.shape
    pixels = height * breadth
    out_count = frame_count // 2
    dp = lax.axis_size("dp")
    x_size = lax.axis_size("x")
    share = channels // dp
    half = share // 2
    core = lax.axis_index("core")
    core_scalar = core[None].astype(jnp.int32)
    frames = clip_frames.reshape(frame_count, pixels, channels)

    cot = cotangent[0].reshape(out_count, pixels, channels)
    following = lax.ppermute(cot[0], ("x", "core"), neighbours(x_size, -1))

    spatial = jnp.concatenate([spatial_weight, time_weight], axis=1)
    spatial_mine = lax.dynamic_slice_in_dim(spatial, core * half, half, axis=0)
    spatial_full = lax.all_gather(spatial_mine, ("dp", "core"), axis=0, tiled=True)
    group = lax.broadcasted_iota(jnp.int32, (channels, channels), 0) // (channels // GROUPS)
    same = (group == group.T).astype(f32)
    held = {}

    def activate(token):
        held["views"], held["mean"], held["scale"] = normalize(
            after(frames, token), same, breadth
        )
        return held["mean"]

    def turn(token):
        held["turned"] = turned_columns(after(held["views"], token))
        return held["turned"][0, :8, :128]

    temporal_full = gather_temporal(temporal_weight, (activate, turn))
    views, mean, scale = held["views"], held["mean"], held["scale"]
    turned = held["turned"].reshape(9, channels, frame_count * pixels)

    embedded = embedding(timesteps[0], time_weight.shape[1])
    hidden_back, back_views, shift_sum = hidden_gradient(cot, following, temporal_full, breadth)
    flat_back = hidden_back.reshape(frame_count * pixels, channels)
    sums = shift_sum
    arriving = flip(sums, "core")

    one = weight_grad(turned, flat_back, 0, dp, core_scalar)
    chain_a = Chain(*one)
    sums = sums + after(arriving, one[1])
    out_a = chain_a.launch()
    for mask in bits_of(x_size):
        arriving = flip(sums, "x", mask)
        sums = sums + after(arriving, out_a)
    pairs = jnp.concatenate([sums, embedded[None]], axis=1)
    two = weight_grad(turned, after(flat_back, out_a), 4, dp, core_scalar)
    chain_a.land(two[1])
    chain_b = Chain(*two)
    out_b = chain_b.launch()
    out_a = chain_a.launch()

    time_full = spatial_full[:, 9 * channels :]
    time_shift = jnp.dot(time_full.astype(f32), embedded, precision=lax.Precision.HIGHEST)
    hidden = conv_forward(views, spatial_full, after(time_shift, out_a, out_b)[None])
    chain_a.land(hidden)
    chain_b.land(hidden)
    before = lax.ppermute(hidden[-1], ("x", "core"), neighbours(x_size, 1))
    out_a = chain_a.launch()
    out_b = chain_b.launch()
    for mask in bits_of(dp):
        pairs = jnp.concatenate([pairs, flip(pairs, "dp", mask)], axis=0)
    last = last_grad(
        turned, flat_back, after(hidden, out_a, out_b), before, cot, dp, core_scalar
    )
    chain_a.land(last[1])
    chain_b.land(last[1])
    chain_c = Chain(*last)
    out_c = chain_c.launch()
    out_a = chain_a.launch()
    out_b = chain_b.launch()

    part = conv_back_start(after(back_views, out_a, out_b, out_c), spatial_full)
    chain_a.land(part)
    chain_b.land(part)
    chain_c.land(part)
    out_c = chain_c.launch()
    first = chain_a.finish()
    out_b = chain_b.launch() if chain_b.stages else out_c
    input_grad = conv_back_end(
        after(back_views, out_c, out_b), spatial_full, part, frames, mean, scale, same
    )
    chain_b.land(input_grad)
    chain_c.land(input_grad)
    out_c = chain_c.launch()
    rows = jnp.stack([first, chain_b.finish()])

    downsampled = temporal_forward(after(hidden, out_c, rows), before, temporal_full)
    chain_c.land(downsampled)
    rows = join_x(rows, downsampled)
    last_rows = join_core(join_x(chain_c.finish()[None]))[0]
    rows = join_core(rows)
    downsampled = downsampled.reshape(1, out_count, height, breadth, channels)
    input_grad = input_grad.reshape(1, frame_count, height, breadth, channels)

    mine = lax.dynamic_slice_in_dim(
        pairs[:, :channels], lax.axis_index("dp") * share, share, axis=1
    )
    time_grad = lax.dot_general(
        mine,
        pairs[:, channels:],
        (((0,), (0,)), ((), ())),
        precision=lax.Precision.HIGHEST,
        preferred_element_type=f32,
    )

    spatial_grad = jnp.concatenate(
        [rows[i, j] for i in range(2) for j in range(4)] + [last_rows[0]], axis=1
    )
    temporal_grad = jnp.concatenate([last_rows[1 + k] for k in range(3)], axis=1)
    return (downsampled, input_grad, spatial_grad, temporal_grad, time_grad)


def solution(mesh):
    dp, tm = mesh.devices.shape
    fine = Mesh(mesh.devices.reshape(dp, tm // 2, 2), ("dp", "x", "core"))
    placed = (
        P("dp", ("x", "core"), None, None, None),
        P("dp", ("x", "core"), None, None, None),
        P("dp"),
        P("dp", None),
        P("dp", None),
        P("dp", None),
    )
    return jax.shard_map(
        body,
        mesh=fine,
        in_specs=placed,
        out_specs=(
            P("dp", ("x", "core"), None, None, None),
            P("dp", ("x", "core"), None, None, None),
            P("dp", None),
            P("dp", None),
            P("dp", None),
        ),
        check_vma=False,
    )
```

```python
import math

import jax
import jax.numpy as jnp
from jax import lax
from jax.experimental import pallas as pl
from jax.experimental.pallas import tpu as pltpu
from jax.sharding import Mesh
from jax.sharding import PartitionSpec as P

GROUPS = 32


epsilon = 1e-05
log_base = math.log(10000.0)
bf16 = jnp.bfloat16
f32 = jnp.float32
VMEM_BYTES = 56 * 1024 * 1024


def embedding(diffusion_step, embed_width):
    half_width = embed_width // 2
    frequency = jnp.exp(-log_base * jnp.arange(half_width, dtype=jnp.float32) / half_width)
    angles = diffusion_step.astype(jnp.float32) * frequency
    return jnp.concatenate([jnp.cos(angles), jnp.sin(angles)])


def flip(x, axis, mask=1):
    count = lax.axis_size(axis)
    return lax.ppermute(x, axis, [(i, i ^ mask) for i in range(count)])


def bits_of(count):
    return [1 << i for i in range(count.bit_length() - 1)]


def params():
    return pltpu.CompilerParams(vmem_limit_bytes=VMEM_BYTES)


def cost(microseconds):
    return pl.CostEstimate(
        flops=int(microseconds * 1.15e9), transcendentals=0, bytes_accessed=int(microseconds * 1e5)
    )


def whole(shape):
    return pl.BlockSpec(shape, lambda *_: (0,) * len(shape), pipeline_mode=pl.Buffered(1))


def is_upper(axis, mask):
    return (lax.axis_index(axis) & mask) != 0


def after(x, *others):
    return lax.optimization_barrier((x,) + others)[0]


def ordered(mine, other, upper, axis):
    low = jnp.where(upper, other, mine)
    high = jnp.where(upper, mine, other)
    return jnp.concatenate([low, high], axis=axis)


def gather_temporal(weight, fillers):
    share, wide = weight.shape
    channels = wide // 3
    half = share // 2
    side = lax.axis_index("x") & 1
    x = lax.dynamic_slice(
        weight, (lax.axis_index("core") * half, side * channels), (half, 2 * channels)
    )
    masks = bits_of(lax.axis_size("dp"))[::-1]
    x = x.reshape((1,) * len(masks) + x.shape)
    for spot, mask in enumerate(masks):
        got = flip(x, "dp", mask)
        if mask == 1:
            got = after(got, fillers[0](x))
        x = ordered(x, got, is_upper("dp", mask), spot)
    upper = side != 0
    low, high = x[..., :channels], x[..., channels:]
    outer = jnp.where(upper, high, low)
    other = after(flip(outer, "x", 1), fillers[1](outer))
    x = jnp.concatenate(
        [jnp.where(upper, other, low), jnp.where(upper, low, high), jnp.where(upper, high, other)],
        axis=-1,
    )
    x = ordered(x, flip(x, "core"), is_upper("core", 1), x.ndim - 2)
    return x.reshape(share * lax.axis_size("dp"), wide)


class Chain:
    def __init__(self, keep, send):
        shards, taps, half, cols = keep.shape
        dp_masks = bits_of(shards)[::-1]
        x_masks = bits_of(lax.axis_size("x"))[::-1]
        nd, nx = len(dp_masks), len(x_masks)
        shape = (2,) * (nd + nx) + (taps >> nx, half, cols)
        self.got = flip(send, "core").reshape(shape)
        self.keep = keep.reshape(shape)
        self.stages = [("x", m, nd + i) for i, m in list(enumerate(x_masks))[::-1]]
        self.stages += [("dp", m, i) for i, m in list(enumerate(dp_masks))[::-1]]

    def launch(self, *tokens):
        if tokens:
            self.got = after(self.got, *tokens)
        axis, mask, spot = self.stages.pop(0)
        bit = is_upper(axis, mask).astype(jnp.int32)

        def pick(which):
            kept = lax.dynamic_index_in_dim(self.keep, which, spot)
            return kept + lax.dynamic_index_in_dim(self.got, which, spot).astype(f32)

        other = pick(1 - bit).astype(bf16)
        self.keep, self.got = pick(bit), flip(other, axis, mask)
        return other

    def land(self, token):
        self.keep, self.got = lax.optimization_barrier((self.keep, self.got, token))[:2]

    def finish(self):
        while self.stages:
            self.launch()
        x = self.keep + self.got.astype(f32)
        return x.reshape(x.shape[-3:])


def join_x(x, token=None):
    for mask in bits_of(lax.axis_size("x")):
        got = flip(x, "x", mask)
        if token is not None:
            x, got = lax.optimization_barrier((x, got, token))[:2]
        x = ordered(x, got, is_upper("x", mask), 1)
    return x


def join_core(x):
    return ordered(x, flip(x, "core"), is_upper("core", 1), 2)


def matmul_nt(a, b):
    return lax.dot_general(a, b, (((1,), (1,)), ((), ())), preferred_element_type=f32)


def matmul_tn(a, b):
    return lax.dot_general(a, b, (((0,), (0,)), ((), ())), preferred_element_type=f32)


def matmul(a, b):
    return jnp.dot(a, b, preferred_element_type=f32)


def group_mean(sums, same_ref, count):
    filled = -(-len(sums) // 8) * 8
    padded = jnp.concatenate(sums + [sums[0]] * (filled - len(sums)), axis=0)
    total = jnp.dot(
        padded, same_ref[...], precision=lax.Precision.HIGHEST, preferred_element_type=f32
    )
    return total * (1.0 / count)


def write_views(ref, frame, values, breadth):
    pixels, channels = values.shape
    height = pixels // breadth
    column = lax.broadcasted_iota(jnp.int32, (pixels, channels), 0) & (breadth - 1)
    left = jnp.where(column == 0, 0.0, pltpu.roll(values, 1, 0))
    right = jnp.where(column == breadth - 1, 0.0, pltpu.roll(values, pixels - 1, 0))
    edge = jnp.zeros((1, breadth, 3 * channels), bf16)
    ref[frame, 0:1] = edge
    ref[frame, height + 1 : height + 2] = edge
    for s, moved in enumerate((left, values, right)):
        ref[frame, 1 : height + 1, :, s * channels : (s + 1) * channels] = moved.astype(
            bf16
        ).reshape(height, breadth, channels)


def rows_of(views_ref, r):
    frames, high, breadth, wide = views_ref.shape
    return views_ref[:, pl.ds(r, high - 2)].reshape(frames * (high - 2) * breadth, wide)


def norm_kernel(count, breadth, x_ref, same_ref, views_ref, mean_ref, scale_ref):
    frames = range(x_ref.shape[0])
    sums = [jnp.sum(x_ref[f].astype(f32), axis=0, keepdims=True) for f in frames]
    centers = group_mean(sums, same_ref, count)
    squares = []
    for f in frames:
        deviation = x_ref[f].astype(f32) - centers[f : f + 1]
        squares.append(jnp.sum(deviation * deviation, axis=0, keepdims=True))
    scales = lax.rsqrt(group_mean(squares, same_ref, count) + epsilon)
    for f in frames:
        center, scaled = centers[f : f + 1], scales[f : f + 1]
        normal = (x_ref[f].astype(f32) - center) * scaled
        mean_ref[f] = center
        scale_ref[f] = scaled
        write_views(views_ref, f, normal / (1.0 + jnp.exp(-normal)), breadth)


def normalize(frames, same, breadth):
    count, pixels, channels = frames.shape
    height = pixels // breadth
    return pl.pallas_call(
        lambda *refs: norm_kernel(pixels * (channels // GROUPS), breadth, *refs),
        out_shape=(
            jax.ShapeDtypeStruct((count, height + 2, breadth, 3 * channels), bf16),
            jax.ShapeDtypeStruct((count, 1, channels), f32),
            jax.ShapeDtypeStruct((count, 1, channels), f32),
        ),
        compiler_params=params(),
        cost_estimate=cost(7.6),
        name="norm",
    )(frames, same)


def turn_kernel(views_ref, out_ref):
    out_ref[0] = rows_of(views_ref, pl.program_id(0)).T


def turned_columns(views):
    frames, high, breadth, wide = views.shape
    rows = frames * (high - 2) * breadth
    return pl.pallas_call(
        turn_kernel,
        grid=(3,),
        in_specs=[whole(views.shape)],
        out_specs=pl.BlockSpec((1, wide, rows), lambda i: (i, 0, 0)),
        out_shape=jax.ShapeDtypeStruct((3, wide, rows), bf16),
        compiler_params=params(),
        cost_estimate=cost(8.5),
        name="turn",
    )(views)


def hidden_grad_kernel(breadth, cot_ref, next_ref, w_ref, back_ref, views_ref, sum_ref):
    outs = cot_ref.shape[0]
    channels = w_ref.shape[0]
    total = jnp.zeros((1, channels), f32)
    for o in range(outs):
        later = cot_ref[o + 1] if o + 1 < outs else next_ref[...]
        even = matmul_nt(cot_ref[o], w_ref[:, channels : 2 * channels])
        odd = matmul_nt(cot_ref[o], w_ref[:, 2 * channels : 3 * channels]) + matmul_nt(
            later, w_ref[:, :channels]
        )
        for frame, values in ((2 * o, even), (2 * o + 1, odd)):
            back_ref[frame] = values.astype(bf16)
            write_views(views_ref, frame, values, breadth)
            total += jnp.sum(values, axis=0, keepdims=True)
    sum_ref[...] = total


def hidden_gradient(cot, following, temporal, breadth):
    outs, pixels, channels = cot.shape
    return pl.pallas_call(
        lambda *refs: hidden_grad_kernel(breadth, *refs),
        out_shape=(
            jax.ShapeDtypeStruct((2 * outs, pixels, channels), bf16),
            jax.ShapeDtypeStruct((2 * outs, pixels // breadth + 2, breadth, 3 * channels), bf16),
            jax.ShapeDtypeStruct((1, channels), f32),
        ),
        compiler_params=params(),
        cost_estimate=cost(6.5),
        name="hidden_grad",
    )(cot, following, temporal)


def store_halves(core_ref, grad, keep_ref, send_ref, slot):
    shards, _, half, channels = keep_ref.shape
    grad = grad.reshape(shards, 2 * half, channels)
    low, high = grad[:, :half], grad[:, half:]

    @pl.when(core_ref[0] == 0)
    def _():
        keep_ref[:, slot] = low
        send_ref[:, slot] = high.astype(bf16)

    @pl.when(core_ref[0] != 0)
    def _():
        keep_ref[:, slot] = high
        send_ref[:, slot] = low.astype(bf16)


def weight_grad_kernel(core_ref, x_ref, back_ref, keep_ref, send_ref):
    store_halves(core_ref, matmul(x_ref[0], back_ref[...]), keep_ref, send_ref, 0)


def weight_grad(turned, hidden_back, first, shards, core):
    rows, channels = hidden_back.shape
    half = channels // shards // 2
    out_spec = pl.BlockSpec((shards, 1, half, channels), lambda i: (0, i, 0, 0))
    return pl.pallas_call(
        weight_grad_kernel,
        grid=(4,),
        in_specs=[
            pl.BlockSpec(memory_space=pltpu.SMEM),
            pl.BlockSpec((1, channels, rows), lambda i: (first + i, 0, 0)),
            whole((rows, channels)),
        ],
        out_specs=(out_spec, out_spec),
        out_shape=(
            jax.ShapeDtypeStruct((shards, 4, half, channels), f32),
            jax.ShapeDtypeStruct((shards, 4, half, channels), bf16),
        ),
        compiler_params=params(),
        cost_estimate=cost(8.5),
        name="weight_grad",
    )(core, turned, hidden_back)


def last_grad_kernel(
    core_ref, x_ref, back_ref, hidden_ref, before_ref, cot_ref, keep_ref, send_ref
):
    store_halves(core_ref, matmul(x_ref[0], back_ref[...]), keep_ref, send_ref, 0)
    for k in range(3):
        grad = 0.0
        for o in range(cot_ref.shape[0]):
            frame = 2 * o + k - 1
            x = before_ref[...] if frame < 0 else hidden_ref[frame]
            grad += matmul_tn(x, cot_ref[o])
        store_halves(core_ref, grad, keep_ref, send_ref, 1 + k)


def last_grad(turned, hidden_back, hidden, before, cot, shards, core):
    rows, channels = hidden_back.shape
    half = channels // shards // 2
    shape = (shards, 4, half, channels)
    return pl.pallas_call(
        last_grad_kernel,
        grid=(1,),
        in_specs=[
            pl.BlockSpec(memory_space=pltpu.SMEM),
            pl.BlockSpec((1, channels, rows), lambda i: (8, 0, 0)),
            whole((rows, channels)),
            whole(hidden.shape),
            whole(before.shape),
            whole(cot.shape),
        ],
        out_specs=(whole(shape), whole(shape)),
        out_shape=(jax.ShapeDtypeStruct(shape, f32), jax.ShapeDtypeStruct(shape, bf16)),
        compiler_params=params(),
        cost_estimate=cost(10.3),
        name="last_grad",
    )(core, turned, hidden_back, hidden, before, cot)


def temporal_kernel(hidden_ref, before_ref, w_ref, out_ref):
    channels = w_ref.shape[0]
    for o in range(out_ref.shape[0]):
        total = 0.0
        for k in range(3):
            frame = 2 * o + k - 1
            x = before_ref[...] if frame < 0 else hidden_ref[frame]
            total += matmul(x, w_ref[:, k * channels : (k + 1) * channels])
        out_ref[o] = total


def temporal_forward(hidden, before, temporal):
    frames, pixels, channels = hidden.shape
    return pl.pallas_call(
        temporal_kernel,
        out_shape=jax.ShapeDtypeStruct((frames // 2, pixels, channels), f32),
        compiler_params=params(),
        cost_estimate=cost(5.2),
        name="temporal",
    )(hidden, before, temporal)


def conv_forward_kernel(views_ref, w_ref, shift_ref, out_ref, acc_ref, tall_ref):
    r = pl.program_id(0)
    rows, channels = acc_ref.shape
    for s in range(3):
        tall_ref[s * channels : (s + 1) * channels] = w_ref[:, s * channels : (s + 1) * channels]
    part = matmul(rows_of(views_ref, r), tall_ref[...])

    @pl.when(r == 0)
    def _():
        acc_ref[...] = part + shift_ref[...]

    @pl.when(r == 1)
    def _():
        acc_ref[...] += part

    @pl.when(r == 2)
    def _():
        out_ref[...] = (acc_ref[...] + part).astype(bf16).reshape(out_ref.shape)


def conv_forward(views, spatial, shift):
    frames, high, breadth, wide = views.shape
    channels = wide // 3
    pixels = (high - 2) * breadth
    return pl.pallas_call(
        conv_forward_kernel,
        grid=(3,),
        in_specs=[
            whole(views.shape),
            pl.BlockSpec((channels, wide), lambda i: (0, i)),
            whole((1, channels)),
        ],
        out_specs=whole((frames, pixels, channels)),
        out_shape=jax.ShapeDtypeStruct((frames, pixels, channels), bf16),
        scratch_shapes=[
            pltpu.VMEM((frames * pixels, channels), f32),
            pltpu.VMEM((wide, channels), bf16),
        ],
        compiler_params=params(),
        cost_estimate=cost(15),
        name="conv_forward",
    )(views, spatial, shift)


def back_part(views_ref, w_ref, r):
    channels = w_ref.shape[0]
    x = rows_of(views_ref, 2 - r)
    x = jnp.concatenate(
        [x[:, (2 - s) * channels : (3 - s) * channels] for s in range(3)], axis=1
    )
    return matmul_nt(x, w_ref[...])


def conv_back_kernel(views_ref, w_ref, acc_ref):
    acc_ref[...] = back_part(views_ref, w_ref, 0)


def conv_back_start(views, spatial):
    frames, high, breadth, wide = views.shape
    channels = wide // 3
    rows = frames * (high - 2) * breadth
    return pl.pallas_call(
        conv_back_kernel,
        grid=(1,),
        in_specs=[whole(views.shape), pl.BlockSpec((channels, wide), lambda i: (0, 0))],
        out_specs=whole((rows, channels)),
        out_shape=jax.ShapeDtypeStruct((rows, channels), f32),
        compiler_params=params(),
        cost_estimate=cost(6.5),
        name="conv_back_start",
    )(views, spatial)


def conv_back_end_kernel(
    count, views_ref, w_ref, part_ref, x_ref, mean_ref, scale_ref, same_ref, out_ref, acc_ref
):
    step = pl.program_id(0)
    part = back_part(views_ref, w_ref, 1 + step)

    @pl.when(step == 0)
    def _():
        acc_ref[...] = part_ref[...] + part

    @pl.when(step == 1)
    def _():
        acc_ref[...] += part
        back_through_norm(count, x_ref, mean_ref, scale_ref, same_ref, out_ref, acc_ref)


def back_through_norm(count, x_ref, mean_ref, scale_ref, same_ref, out_ref, acc_ref):
    frames, pixels, _ = x_ref.shape

    def parts(f):
        normal = (x_ref[f].astype(f32) - mean_ref[f]) * scale_ref[f]
        gate = 1.0 / (1.0 + jnp.exp(-normal))
        slope = gate * (1.0 + normal * (1.0 - gate))
        return normal, slope

    sums = []
    for f in range(frames):
        normal, slope = parts(f)
        grad = acc_ref[f * pixels : (f + 1) * pixels] * slope
        acc_ref[f * pixels : (f + 1) * pixels] = grad
        sums.append(jnp.sum(grad, axis=0, keepdims=True))
        sums.append(jnp.sum(grad * normal, axis=0, keepdims=True))
    means = group_mean(sums, same_ref, count)
    for f in range(frames):
        normal = (x_ref[f].astype(f32) - mean_ref[f]) * scale_ref[f]
        one, two = means[2 * f : 2 * f + 1], means[2 * f + 1 : 2 * f + 2]
        grad = acc_ref[f * pixels : (f + 1) * pixels]
        out_ref[f] = (grad - one - normal * two) * scale_ref[f]


def conv_back_end(views, spatial, part, frames, mean, scale, same):
    count, pixels, channels = frames.shape
    return pl.pallas_call(
        lambda *refs: conv_back_end_kernel(pixels * (channels // GROUPS), *refs),
        grid=(2,),
        in_specs=[
            whole(views.shape),
            pl.BlockSpec((channels, 3 * channels), lambda i: (0, 1 + i)),
            whole(part.shape),
            whole(frames.shape),
            whole(mean.shape),
            whole(scale.shape),
            whole(same.shape),
        ],
        out_specs=whole(frames.shape),
        out_shape=jax.ShapeDtypeStruct(frames.shape, f32),
        scratch_shapes=[pltpu.VMEM((count * pixels, channels), f32)],
        compiler_params=params(),
        cost_estimate=cost(18),
        name="conv_back_end",
    )(views, spatial, part, frames, mean, scale, same)


def neighbours(x_size, step):
    count = 2 * x_size
    return [(i, i + step) for i in range(count) if 0 <= i + step < count]


def body(latents, cotangent, timesteps, spatial_weight, temporal_weight, time_weight):
    clip_frames = latents[0]
    frame_count, height, breadth, channels = clip_frames.shape
    pixels = height * breadth
    out_count = frame_count // 2
    dp = lax.axis_size("dp")
    x_size = lax.axis_size("x")
    share = channels // dp
    half = share // 2
    core = lax.axis_index("core")
    core_scalar = core[None].astype(jnp.int32)
    frames = clip_frames.reshape(frame_count, pixels, channels)

    cot = cotangent[0].reshape(out_count, pixels, channels)
    following = lax.ppermute(cot[0], ("x", "core"), neighbours(x_size, -1))

    spatial = jnp.concatenate([spatial_weight, time_weight], axis=1)
    spatial_mine = lax.dynamic_slice_in_dim(spatial, core * half, half, axis=0)
    spatial_full = lax.all_gather(spatial_mine, ("dp", "core"), axis=0, tiled=True)
    group = lax.broadcasted_iota(jnp.int32, (channels, channels), 0) // (channels // GROUPS)
    same = (group == group.T).astype(f32)
    held = {}

    def activate(token):
        held["views"], held["mean"], held["scale"] = normalize(
            after(frames, token), same, breadth
        )
        return held["mean"]

    def turn(token):
        held["turned"] = turned_columns(after(held["views"], token))
        return held["turned"]

    temporal_full = gather_temporal(temporal_weight, (activate, turn))
    views, mean, scale = held["views"], held["mean"], held["scale"]
    turned = held["turned"].reshape(9, channels, frame_count * pixels)

    embedded = embedding(timesteps[0], time_weight.shape[1])
    hidden_back, back_views, shift_sum = hidden_gradient(cot, following, temporal_full, breadth)
    flat_back = hidden_back.reshape(frame_count * pixels, channels)
    sums = shift_sum
    arriving = flip(sums, "core")

    one = weight_grad(turned, flat_back, 0, dp, core_scalar)
    chain_a = Chain(*one)
    sums = sums + after(arriving, one[1])
    arriving = flip(sums, "x", 1)
    two = weight_grad(turned, after(flat_back, sums), 4, dp, core_scalar)
    sums = sums + after(arriving, two[1])
    for mask in bits_of(x_size)[1:]:
        sums = sums + flip(sums, "x", mask)
    pairs = jnp.concatenate([sums, embedded[None]], axis=1)
    steps = bits_of(dp)
    arriving = flip(pairs, "dp", steps.pop(0))
    chain_a.land(two[1])
    chain_b = Chain(*two)
    out_a = chain_a.launch()

    time_full = spatial_full[:, 9 * channels :]
    time_shift = jnp.dot(time_full.astype(f32), embedded, precision=lax.Precision.HIGHEST)
    hidden = conv_forward(views, spatial_full, after(time_shift, out_a, pairs)[None])
    pairs = jnp.concatenate([pairs, after(arriving, hidden)], axis=0)
    arriving = flip(pairs, "dp", steps.pop(0))
    chain_a.land(hidden)
    chain_b.land(hidden)
    before = lax.ppermute(hidden[-1], ("x", "core"), neighbours(x_size, 1))
    out_a = chain_a.launch()
    out_b = chain_b.launch(before)
    last = last_grad(
        turned, flat_back, after(hidden, out_a, out_b, pairs), before, cot, dp, core_scalar
    )
    pairs = jnp.concatenate([pairs, after(arriving, last[1])], axis=0)
    arriving = flip(pairs, "dp", steps.pop(0))
    chain_a.land(last[1])
    chain_b.land(last[1])
    chain_c = Chain(*last)
    out_a = chain_a.launch()
    out_b = chain_b.launch()

    part = conv_back_start(after(back_views, out_a, out_b, pairs), spatial_full)
    pairs = jnp.concatenate([pairs, after(arriving, part)], axis=0)
    for mask in steps:
        pairs = jnp.concatenate([pairs, flip(pairs, "dp", mask)], axis=0)
    chain_a.land(part)
    chain_b.land(part)
    chain_c.land(part)
    out_c = chain_c.launch()
    out_a = chain_a.launch()
    out_b = chain_b.launch()
    input_grad = conv_back_end(
        after(back_views, out_a, out_b, out_c), spatial_full, part, frames, mean, scale, same
    )
    chain_a.land(input_grad)
    chain_b.land(input_grad)
    chain_c.land(input_grad)
    out_c = chain_c.launch()
    first = chain_a.finish()
    out_b = chain_b.launch()

    downsampled = temporal_forward(after(hidden, first, out_b, out_c), before, temporal_full)
    chain_b.land(downsampled)
    chain_c.land(downsampled)
    out_c = chain_c.launch()
    rows = join_x(jnp.stack([first, chain_b.finish()]))
    last_rows = join_core(join_x(chain_c.finish()[None]))[0]
    rows = join_core(rows)
    downsampled = downsampled.reshape(1, out_count, height, breadth, channels)
    input_grad = input_grad.reshape(1, frame_count, height, breadth, channels)

    mine = lax.dynamic_slice_in_dim(
        pairs[:, :channels], lax.axis_index("dp") * share, share, axis=1
    )
    time_grad = lax.dot_general(
        mine,
        pairs[:, channels:],
        (((0,), (0,)), ((), ())),
        precision=lax.Precision.HIGHEST,
        preferred_element_type=f32,
    )

    spatial_grad = jnp.concatenate(
        [rows[i, j] for i in range(2) for j in range(4)] + [last_rows[0]], axis=1
    )
    temporal_grad = jnp.concatenate([last_rows[1 + k] for k in range(3)], axis=1)
    return (downsampled, input_grad, spatial_grad, temporal_grad, time_grad)


def solution(mesh):
    dp, tm = mesh.devices.shape
    fine = Mesh(mesh.devices.reshape(dp, tm // 2, 2), ("dp", "x", "core"))
    placed = (
        P("dp", ("x", "core"), None, None, None),
        P("dp", ("x", "core"), None, None, None),
        P("dp"),
        P("dp", None),
        P("dp", None),
        P("dp", None),
    )
    return jax.shard_map(
        body,
        mesh=fine,
        in_specs=placed,
        out_specs=(
            P("dp", ("x", "core"), None, None, None),
            P("dp", ("x", "core"), None, None, None),
            P("dp", None),
            P("dp", None),
            P("dp", None),
        ),
        check_vma=False,
    )
```

```python
import math

import jax
import jax.numpy as jnp
from jax import lax
from jax.experimental import pallas as pl
from jax.experimental.pallas import tpu as pltpu
from jax.sharding import Mesh
from jax.sharding import PartitionSpec as P

GROUPS = 32


epsilon = 1e-05
log_base = math.log(10000.0)
bf16 = jnp.bfloat16
f32 = jnp.float32
VMEM_BYTES = 56 * 1024 * 1024
PAIR_WIDTH = 8960


def embedding(diffusion_step, embed_width):
    half_width = embed_width // 2
    frequency = jnp.exp(-log_base * jnp.arange(half_width, dtype=jnp.float32) / half_width)
    angles = diffusion_step.astype(jnp.float32) * frequency
    return jnp.concatenate([jnp.cos(angles), jnp.sin(angles)])


def flip(x, axis, mask=1):
    count = lax.axis_size(axis)
    return lax.ppermute(x, axis, [(i, i ^ mask) for i in range(count)])


def bits_of(count):
    return [1 << i for i in range(count.bit_length() - 1)]


def params():
    return pltpu.CompilerParams(vmem_limit_bytes=VMEM_BYTES)


def cost(microseconds):
    return pl.CostEstimate(
        flops=int(microseconds * 1.15e9), transcendentals=0, bytes_accessed=int(microseconds * 1e5)
    )


def whole(shape):
    return pl.BlockSpec(shape, lambda *_: (0,) * len(shape), pipeline_mode=pl.Buffered(1))


def is_upper(axis, mask):
    return (lax.axis_index(axis) & mask) != 0


def after(x, *others):
    return lax.optimization_barrier((x,) + others)[0]


def ordered(mine, other, upper, axis):
    low = jnp.where(upper, other, mine)
    high = jnp.where(upper, mine, other)
    return jnp.concatenate([low, high], axis=axis)


def gather_temporal(weight, fillers):
    share, wide = weight.shape
    channels = wide // 3
    half = share // 2
    side = lax.axis_index("x") & 1
    x = lax.dynamic_slice(
        weight, (lax.axis_index("core") * half, side * channels), (half, 2 * channels)
    )
    masks = bits_of(lax.axis_size("dp"))[::-1]
    x = x.reshape((1,) * len(masks) + x.shape)
    for spot, mask in enumerate(masks):
        got = flip(x, "dp", mask)
        if mask == 1:
            got = after(got, fillers[0](x))
        x = ordered(x, got, is_upper("dp", mask), spot)
    upper = side != 0
    low, high = x[..., :channels], x[..., channels:]
    outer = jnp.where(upper, high, low)
    other = after(flip(outer, "x", 1), fillers[1](outer))
    x = jnp.concatenate(
        [jnp.where(upper, other, low), jnp.where(upper, low, high), jnp.where(upper, high, other)],
        axis=-1,
    )
    x = ordered(x, flip(x, "core"), is_upper("core", 1), x.ndim - 2)
    return x.reshape(share * lax.axis_size("dp"), wide)


class Chain:
    def __init__(self, keep, *sends):
        shards, taps, half, cols = keep.shape
        dp_masks = bits_of(shards)[::-1]
        x_masks = bits_of(lax.axis_size("x"))[::-1]
        nd, nx = len(dp_masks), len(x_masks)
        shape = (2,) * (nd + nx) + (taps >> nx, half, cols)
        gots = [flip(send, "core") for send in sends]
        if len(gots) == 1:
            self.got, self.pair = gots[0].reshape(shape), None
        else:
            shape_of_one = shape[:nd] + (1,) + shape[nd + 1 :]
            self.got, self.pair = (got.reshape(shape_of_one) for got in gots)
        self.keep = keep.reshape(shape)
        self.stages = [("x", m, nd + i) for i, m in enumerate(x_masks)]
        self.stages += [("dp", m, i) for i, m in list(enumerate(dp_masks))[::-1]]

    def launch(self, *tokens):
        if tokens:
            self.got = after(self.got, *tokens)
        axis, mask, spot = self.stages.pop(0)
        bit = is_upper(axis, mask).astype(jnp.int32)

        def pick(which):
            kept = lax.dynamic_index_in_dim(self.keep, which, spot)
            if self.pair is not None:
                return kept + jnp.where(which != 0, self.pair, self.got).astype(f32)
            return kept + lax.dynamic_index_in_dim(self.got, which, spot).astype(f32)

        other = pick(1 - bit).astype(bf16)
        self.keep, self.got, self.pair = pick(bit), flip(other, axis, mask), None
        return other

    def land(self, token):
        self.keep, self.got = lax.optimization_barrier((self.keep, self.got, token))[:2]

    def finish(self):
        while self.stages:
            self.launch()
        x = self.keep + self.got.astype(f32)
        return x.reshape(x.shape[-3:])


def join_x(x, token=None):
    for mask in bits_of(lax.axis_size("x")):
        got = flip(x, "x", mask)
        if token is not None:
            x, got = lax.optimization_barrier((x, got, token))[:2]
        x = ordered(x, got, is_upper("x", mask), 1)
    return x


def join_core(x):
    return ordered(x, flip(x, "core"), is_upper("core", 1), 2)


def matmul_nt(a, b):
    return lax.dot_general(a, b, (((1,), (1,)), ((), ())), preferred_element_type=f32)


def matmul_tn(a, b):
    return lax.dot_general(a, b, (((0,), (0,)), ((), ())), preferred_element_type=f32)


def matmul(a, b):
    return jnp.dot(a, b, preferred_element_type=f32)


def group_mean(sums, same_ref, count):
    filled = -(-len(sums) // 8) * 8
    padded = jnp.concatenate(sums + [sums[0]] * (filled - len(sums)), axis=0)
    total = jnp.dot(
        padded, same_ref[...], precision=lax.Precision.HIGHEST, preferred_element_type=f32
    )
    return total * (1.0 / count)


def write_views(ref, frame, values, breadth):
    pixels, channels = values.shape
    height = pixels // breadth
    column = lax.broadcasted_iota(jnp.int32, (pixels, channels), 0) & (breadth - 1)
    left = jnp.where(column == 0, 0.0, pltpu.roll(values, 1, 0))
    right = jnp.where(column == breadth - 1, 0.0, pltpu.roll(values, pixels - 1, 0))
    edge = jnp.zeros((1, breadth, 3 * channels), bf16)
    ref[frame, 0:1] = edge
    ref[frame, height + 1 : height + 2] = edge
    for s, moved in enumerate((left, values, right)):
        ref[frame, 1 : height + 1, :, s * channels : (s + 1) * channels] = moved.astype(
            bf16
        ).reshape(height, breadth, channels)


def rows_of(views_ref, r):
    frames, high, breadth, wide = views_ref.shape
    return views_ref[:, pl.ds(r, high - 2)].reshape(frames * (high - 2) * breadth, wide)


def norm_kernel(count, breadth, x_ref, same_ref, views_ref, mean_ref, scale_ref):
    frames = range(x_ref.shape[0])
    sums = [jnp.sum(x_ref[f].astype(f32), axis=0, keepdims=True) for f in frames]
    centers = group_mean(sums, same_ref, count)
    squares = []
    for f in frames:
        deviation = x_ref[f].astype(f32) - centers[f : f + 1]
        squares.append(jnp.sum(deviation * deviation, axis=0, keepdims=True))
    scales = lax.rsqrt(group_mean(squares, same_ref, count) + epsilon)
    for f in frames:
        center, scaled = centers[f : f + 1], scales[f : f + 1]
        normal = (x_ref[f].astype(f32) - center) * scaled
        mean_ref[f] = center
        scale_ref[f] = scaled
        write_views(views_ref, f, normal / (1.0 + jnp.exp(-normal)), breadth)


def normalize(frames, same, breadth):
    count, pixels, channels = frames.shape
    height = pixels // breadth
    return pl.pallas_call(
        lambda *refs: norm_kernel(pixels * (channels // GROUPS), breadth, *refs),
        out_shape=(
            jax.ShapeDtypeStruct((count, height + 2, breadth, 3 * channels), bf16),
            jax.ShapeDtypeStruct((count, 1, channels), f32),
            jax.ShapeDtypeStruct((count, 1, channels), f32),
        ),
        compiler_params=params(),
        cost_estimate=cost(7.6),
        name="norm",
    )(frames, same)


def turn_kernel(views_ref, out_ref):
    out_ref[0] = rows_of(views_ref, pl.program_id(0)).T


def turned_columns(views):
    frames, high, breadth, wide = views.shape
    rows = frames * (high - 2) * breadth
    return pl.pallas_call(
        turn_kernel,
        grid=(3,),
        in_specs=[whole(views.shape)],
        out_specs=pl.BlockSpec((1, wide, rows), lambda i: (i, 0, 0)),
        out_shape=jax.ShapeDtypeStruct((3, wide, rows), bf16),
        compiler_params=params(),
        cost_estimate=cost(8.5),
        name="turn",
    )(views)


def hidden_grad_kernel(breadth, cot_ref, next_ref, w_ref, back_ref, views_ref, sum_ref):
    outs = cot_ref.shape[0]
    channels = w_ref.shape[0]
    total = jnp.zeros((1, channels), f32)
    for o in range(outs):
        later = cot_ref[o + 1] if o + 1 < outs else next_ref[...]
        even = matmul_nt(cot_ref[o], w_ref[:, channels : 2 * channels])
        odd = matmul_nt(cot_ref[o], w_ref[:, 2 * channels : 3 * channels]) + matmul_nt(
            later, w_ref[:, :channels]
        )
        for frame, values in ((2 * o, even), (2 * o + 1, odd)):
            back_ref[frame] = values.astype(bf16)
            write_views(views_ref, frame, values, breadth)
            total += jnp.sum(values, axis=0, keepdims=True)
    sum_ref[...] = total


def hidden_gradient(cot, following, temporal, breadth):
    outs, pixels, channels = cot.shape
    return pl.pallas_call(
        lambda *refs: hidden_grad_kernel(breadth, *refs),
        out_shape=(
            jax.ShapeDtypeStruct((2 * outs, pixels, channels), bf16),
            jax.ShapeDtypeStruct((2 * outs, pixels // breadth + 2, breadth, 3 * channels), bf16),
            jax.ShapeDtypeStruct((1, channels), f32),
        ),
        compiler_params=params(),
        cost_estimate=cost(6.5),
        name="hidden_grad",
    )(cot, following, temporal)


def store_halves(core_ref, grad, keep_ref, send_ref, slot, send_slot):
    shards, _, half, channels = keep_ref.shape
    grad = grad.reshape(shards, 2 * half, channels)
    low, high = grad[:, :half], grad[:, half:]

    @pl.when(core_ref[0] == 0)
    def _():
        keep_ref[:, slot] = low
        send_ref[:, send_slot] = high.astype(bf16)

    @pl.when(core_ref[0] != 0)
    def _():
        keep_ref[:, slot] = high
        send_ref[:, send_slot] = low.astype(bf16)


def weight_grad_kernel(core_ref, x_ref, back_ref, keep_ref, send_ref):
    store_halves(core_ref, matmul(x_ref[0], back_ref[...]), keep_ref, send_ref, 0, 0)


def weight_grad(turned, hidden_back, first, shards, core):
    rows, channels = hidden_back.shape
    half = channels // shards // 2
    out_spec = pl.BlockSpec((shards, 1, half, channels), lambda i: (0, i, 0, 0))
    return pl.pallas_call(
        weight_grad_kernel,
        grid=(4,),
        in_specs=[
            pl.BlockSpec(memory_space=pltpu.SMEM),
            pl.BlockSpec((1, channels, rows), lambda i: (first + i, 0, 0)),
            whole((rows, channels)),
        ],
        out_specs=(out_spec, out_spec),
        out_shape=(
            jax.ShapeDtypeStruct((shards, 4, half, channels), f32),
            jax.ShapeDtypeStruct((shards, 4, half, channels), bf16),
        ),
        compiler_params=params(),
        cost_estimate=cost(8.5),
        name="weight_grad",
    )(core, turned, hidden_back)


def last_grad_kernel(
    core_ref, x_ref, back_ref, hidden_ref, before_ref, cot_ref, keep_ref, one_ref, two_ref
):
    sends = ((one_ref, 0), (one_ref, 1), (two_ref, 0), (two_ref, 1))
    grad = matmul(x_ref[0], back_ref[...])
    store_halves(core_ref, grad, keep_ref, sends[0][0], 0, sends[0][1])
    for k in range(3):
        grad = 0.0
        for o in range(cot_ref.shape[0]):
            frame = 2 * o + k - 1
            x = before_ref[...] if frame < 0 else hidden_ref[frame]
            grad += matmul_tn(x, cot_ref[o])
        store_halves(core_ref, grad, keep_ref, sends[1 + k][0], 1 + k, sends[1 + k][1])


def last_grad(turned, hidden_back, hidden, before, cot, shards, core):
    rows, channels = hidden_back.shape
    half = channels // shards // 2
    shape = (shards, 4, half, channels)
    two = (shards, 2, half, channels)
    return pl.pallas_call(
        last_grad_kernel,
        grid=(1,),
        in_specs=[
            pl.BlockSpec(memory_space=pltpu.SMEM),
            pl.BlockSpec((1, channels, rows), lambda i: (8, 0, 0)),
            whole((rows, channels)),
            whole(hidden.shape),
            whole(before.shape),
            whole(cot.shape),
        ],
        out_specs=(whole(shape), whole(two), whole(two)),
        out_shape=(
            jax.ShapeDtypeStruct(shape, f32),
            jax.ShapeDtypeStruct(two, bf16),
            jax.ShapeDtypeStruct(two, bf16),
        ),
        compiler_params=params(),
        cost_estimate=cost(10.3),
        name="last_grad",
    )(core, turned, hidden_back, hidden, before, cot)


def temporal_kernel(hidden_ref, before_ref, w_ref, out_ref):
    channels = w_ref.shape[0]
    for o in range(out_ref.shape[0]):
        total = 0.0
        for k in range(3):
            frame = 2 * o + k - 1
            x = before_ref[...] if frame < 0 else hidden_ref[frame]
            total += matmul(x, w_ref[:, k * channels : (k + 1) * channels])
        out_ref[o] = total


def temporal_forward(hidden, before, temporal):
    frames, pixels, channels = hidden.shape
    return pl.pallas_call(
        temporal_kernel,
        out_shape=jax.ShapeDtypeStruct((frames // 2, pixels, channels), f32),
        compiler_params=params(),
        cost_estimate=cost(5.2),
        name="temporal",
    )(hidden, before, temporal)


def conv_forward_kernel(views_ref, w_ref, shift_ref, out_ref, last_ref, acc_ref, tall_ref):
    r = pl.program_id(0)
    rows, channels = acc_ref.shape
    for s in range(3):
        tall_ref[s * channels : (s + 1) * channels] = w_ref[:, s * channels : (s + 1) * channels]
    part = matmul(rows_of(views_ref, r), tall_ref[...])

    @pl.when(r == 0)
    def _():
        acc_ref[...] = part + shift_ref[...]

    @pl.when(r == 1)
    def _():
        acc_ref[...] += part

    @pl.when(r == 2)
    def _():
        hidden = (acc_ref[...] + part).astype(bf16).reshape(out_ref.shape)
        out_ref[...] = hidden
        last_ref[...] = hidden[-1]


def conv_forward(views, spatial, shift):
    frames, high, breadth, wide = views.shape
    channels = wide // 3
    pixels = (high - 2) * breadth
    return pl.pallas_call(
        conv_forward_kernel,
        grid=(3,),
        in_specs=[
            whole(views.shape),
            pl.BlockSpec((channels, wide), lambda i: (0, i)),
            whole((1, channels)),
        ],
        out_specs=(whole((frames, pixels, channels)), whole((pixels, channels))),
        out_shape=(
            jax.ShapeDtypeStruct((frames, pixels, channels), bf16),
            jax.ShapeDtypeStruct((pixels, channels), bf16),
        ),
        scratch_shapes=[
            pltpu.VMEM((frames * pixels, channels), f32),
            pltpu.VMEM((wide, channels), bf16),
        ],
        compiler_params=params(),
        cost_estimate=cost(15),
        name="conv_forward",
    )(views, spatial, shift)


def back_part(views_ref, w_ref, r):
    channels = w_ref.shape[0]
    x = rows_of(views_ref, 2 - r)
    x = jnp.concatenate(
        [x[:, (2 - s) * channels : (3 - s) * channels] for s in range(3)], axis=1
    )
    return matmul_nt(x, w_ref[...])


def conv_back_kernel(views_ref, w_ref, acc_ref):
    r = pl.program_id(0)
    part = back_part(views_ref, w_ref, r)

    @pl.when(r == 0)
    def _():
        acc_ref[...] = part

    @pl.when(r != 0)
    def _():
        acc_ref[...] += part


def conv_back_start(views, spatial):
    frames, high, breadth, wide = views.shape
    channels = wide // 3
    rows = frames * (high - 2) * breadth
    return pl.pallas_call(
        conv_back_kernel,
        grid=(2,),
        in_specs=[whole(views.shape), pl.BlockSpec((channels, wide), lambda i: (0, i))],
        out_specs=whole((rows, channels)),
        out_shape=jax.ShapeDtypeStruct((rows, channels), f32),
        compiler_params=params(),
        cost_estimate=cost(12),
        name="conv_back_start",
    )(views, spatial)


def conv_back_end_kernel(
    count, views_ref, w_ref, part_ref, x_ref, mean_ref, scale_ref, same_ref, out_ref, acc_ref
):
    acc_ref[...] = part_ref[...] + back_part(views_ref, w_ref, 2)
    back_through_norm(count, x_ref, mean_ref, scale_ref, same_ref, out_ref, acc_ref)


def back_through_norm(count, x_ref, mean_ref, scale_ref, same_ref, out_ref, acc_ref):
    frames, pixels, _ = x_ref.shape

    def parts(f):
        normal = (x_ref[f].astype(f32) - mean_ref[f]) * scale_ref[f]
        gate = 1.0 / (1.0 + jnp.exp(-normal))
        slope = gate * (1.0 + normal * (1.0 - gate))
        return normal, slope

    sums = []
    for f in range(frames):
        normal, slope = parts(f)
        grad = acc_ref[f * pixels : (f + 1) * pixels] * slope
        acc_ref[f * pixels : (f + 1) * pixels] = grad
        sums.append(jnp.sum(grad, axis=0, keepdims=True))
        sums.append(jnp.sum(grad * normal, axis=0, keepdims=True))
    means = group_mean(sums, same_ref, count)
    for f in range(frames):
        normal = (x_ref[f].astype(f32) - mean_ref[f]) * scale_ref[f]
        one, two = means[2 * f : 2 * f + 1], means[2 * f + 1 : 2 * f + 2]
        grad = acc_ref[f * pixels : (f + 1) * pixels]
        out_ref[f] = (grad - one - normal * two) * scale_ref[f]


def conv_back_end(views, spatial, part, frames, mean, scale, same):
    count, pixels, channels = frames.shape
    return pl.pallas_call(
        lambda *refs: conv_back_end_kernel(pixels * (channels // GROUPS), *refs),
        grid=(1,),
        in_specs=[
            whole(views.shape),
            pl.BlockSpec((channels, 3 * channels), lambda i: (0, 2)),
            whole(part.shape),
            whole(frames.shape),
            whole(mean.shape),
            whole(scale.shape),
            whole(same.shape),
        ],
        out_specs=whole(frames.shape),
        out_shape=jax.ShapeDtypeStruct(frames.shape, f32),
        scratch_shapes=[pltpu.VMEM((count * pixels, channels), f32)],
        compiler_params=params(),
        cost_estimate=cost(12),
        name="conv_back_end",
    )(views, spatial, part, frames, mean, scale, same)


def neighbours(x_size, step):
    count = 2 * x_size
    return [(i, i + step) for i in range(count) if 0 <= i + step < count]


def body(latents, cotangent, timesteps, spatial_weight, temporal_weight, time_weight):
    clip_frames = latents[0]
    frame_count, height, breadth, channels = clip_frames.shape
    pixels = height * breadth
    out_count = frame_count // 2
    dp = lax.axis_size("dp")
    x_size = lax.axis_size("x")
    share = channels // dp
    half = share // 2
    core = lax.axis_index("core")
    core_scalar = core[None].astype(jnp.int32)
    frames = clip_frames.reshape(frame_count, pixels, channels)

    cot = cotangent[0].reshape(out_count, pixels, channels)
    following = lax.ppermute(cot[0], ("x", "core"), neighbours(x_size, -1))

    spatial = jnp.concatenate([spatial_weight, time_weight], axis=1)
    spatial_mine = lax.dynamic_slice_in_dim(spatial, core * half, half, axis=0)
    spatial_full = lax.all_gather(spatial_mine, ("dp", "core"), axis=0, tiled=True)
    group = lax.broadcasted_iota(jnp.int32, (channels, channels), 0) // (channels // GROUPS)
    same = (group == group.T).astype(f32)
    held = {}

    def activate(token):
        held["views"], held["mean"], held["scale"] = normalize(
            after(frames, token), same, breadth
        )
        return held["mean"]

    def turn(token):
        held["turned"] = turned_columns(after(held["views"], token))
        return held["turned"]

    temporal_full = gather_temporal(temporal_weight, (activate, turn))
    views, mean, scale = held["views"], held["mean"], held["scale"]
    turned = held["turned"].reshape(9, channels, frame_count * pixels)

    embedded = embedding(timesteps[0], time_weight.shape[1])
    hidden_back, back_views, shift_sum = hidden_gradient(cot, following, temporal_full, breadth)
    flat_back = hidden_back.reshape(frame_count * pixels, channels)
    pairs = jnp.concatenate([shift_sum, embedded[None]], axis=1)
    pairs = jnp.pad(pairs, ((0, 0), (0, PAIR_WIDTH - pairs.shape[1])))
    pairs = lax.all_gather(pairs, ("dp", "x", "core"), axis=0, tiled=True)

    one = weight_grad(turned, flat_back, 0, dp, core_scalar)
    chain_a = Chain(*one)
    two = weight_grad(turned, flat_back, 4, dp, core_scalar)
    chain_a.land(two[1])
    chain_b = Chain(*two)
    out_a = chain_a.launch()

    time_full = spatial_full[:, 9 * channels :]
    time_shift = jnp.dot(time_full.astype(f32), embedded, precision=lax.Precision.HIGHEST)
    hidden, end = conv_forward(views, spatial_full, after(time_shift, out_a)[None])
    chain_a.land(hidden)
    chain_b.land(hidden)
    before = lax.ppermute(end, ("x", "core"), neighbours(x_size, 1))
    out_a = chain_a.launch()
    out_b = chain_b.launch(before)
    last = last_grad(turned, flat_back, after(hidden, out_a, out_b), before, cot, dp, core_scalar)
    chain_a.land(last[1])
    chain_b.land(last[1])
    chain_c = Chain(*last)
    out_a = chain_a.launch()
    out_b = chain_b.launch(out_a)
    out_c = chain_c.launch(out_b)

    part = conv_back_start(after(back_views, out_c), spatial_full)
    chain_a.land(part)
    chain_b.land(part)
    chain_c.land(part)
    out_a = chain_a.launch()
    out_b = chain_b.launch(out_a)
    out_c = chain_c.launch(out_b)
    input_grad = conv_back_end(
        after(back_views, out_c), spatial_full, part, frames, mean, scale, same
    )
    chain_a.land(input_grad)
    chain_b.land(input_grad)
    chain_c.land(input_grad)
    out_c = chain_c.launch()
    first = chain_a.finish()
    out_b = chain_b.launch(out_c)

    downsampled = temporal_forward(after(hidden, first, out_b), before, temporal_full)
    chain_b.land(downsampled)
    chain_c.land(downsampled)
    out_c = chain_c.launch()
    rows = join_x(jnp.stack([first, after(chain_b.finish(), out_c)]))
    last_rows = join_core(join_x(chain_c.finish()[None]))[0]
    rows = join_core(rows)
    downsampled = downsampled.reshape(1, out_count, height, breadth, channels)
    input_grad = input_grad.reshape(1, frame_count, height, breadth, channels)

    mine = lax.dynamic_slice_in_dim(
        pairs[:, :channels], lax.axis_index("dp") * share, share, axis=1
    )
    time_grad = lax.dot_general(
        mine,
        pairs[:, channels : channels + time_weight.shape[1]],
        (((0,), (0,)), ((), ())),
        precision=lax.Precision.HIGHEST,
        preferred_element_type=f32,
    )

    spatial_grad = jnp.concatenate(
        [rows[i, j] for i in range(2) for j in range(4)] + [last_rows[0]], axis=1
    )
    temporal_grad = jnp.concatenate([last_rows[1 + k] for k in range(3)], axis=1)
    return (downsampled, input_grad, spatial_grad, temporal_grad, time_grad)


def solution(mesh):
    dp, tm = mesh.devices.shape
    fine = Mesh(mesh.devices.reshape(dp, tm // 2, 2), ("dp", "x", "core"))
    placed = (
        P("dp", ("x", "core"), None, None, None),
        P("dp", ("x", "core"), None, None, None),
        P("dp"),
        P("dp", None),
        P("dp", None),
        P("dp", None),
    )
    return jax.shard_map(
        body,
        mesh=fine,
        in_specs=placed,
        out_specs=(
            P("dp", ("x", "core"), None, None, None),
            P("dp", ("x", "core"), None, None, None),
            P("dp", None),
            P("dp", None),
            P("dp", None),
        ),
        check_vma=False,
    )
```

```python
import math

import jax
import jax.numpy as jnp
from jax import lax
from jax.experimental import pallas as pl
from jax.experimental.pallas import tpu as pltpu
from jax.sharding import Mesh
from jax.sharding import PartitionSpec as P

GROUPS = 32


epsilon = 1e-05
log_base = math.log(10000.0)
bf16 = jnp.bfloat16
f32 = jnp.float32
VMEM_BYTES = 56 * 1024 * 1024
PAIR_WIDTH = 8960


def embedding(diffusion_step, embed_width):
    half_width = embed_width // 2
    frequency = jnp.exp(-log_base * jnp.arange(half_width, dtype=jnp.float32) / half_width)
    angles = diffusion_step.astype(jnp.float32) * frequency
    return jnp.concatenate([jnp.cos(angles), jnp.sin(angles)])


def flip(x, axis, mask=1):
    count = lax.axis_size(axis)
    return lax.ppermute(x, axis, [(i, i ^ mask) for i in range(count)])


def bits_of(count):
    return [1 << i for i in range(count.bit_length() - 1)]


def params(size=VMEM_BYTES):
    return pltpu.CompilerParams(vmem_limit_bytes=size)


def cost(microseconds):
    return pl.CostEstimate(
        flops=int(microseconds * 1.15e9), transcendentals=0, bytes_accessed=int(microseconds * 1e5)
    )


def whole(shape):
    return pl.BlockSpec(shape, lambda *_: (0,) * len(shape), pipeline_mode=pl.Buffered(1))


def is_upper(axis, mask):
    return (lax.axis_index(axis) & mask) != 0


def after(x, *others):
    return lax.optimization_barrier((x,) + others)[0]


def ordered(mine, other, upper, axis):
    low = jnp.where(upper, other, mine)
    high = jnp.where(upper, mine, other)
    return jnp.concatenate([low, high], axis=axis)


def gather_temporal(weight, fillers):
    share, wide = weight.shape
    channels = wide // 3
    half = share // 2
    side = lax.axis_index("x") & 1
    x = lax.dynamic_slice(
        weight, (lax.axis_index("core") * half, side * channels), (half, 2 * channels)
    )
    masks = bits_of(lax.axis_size("dp"))[::-1]
    x = x.reshape((1,) * len(masks) + x.shape)
    for spot, mask in enumerate(masks):
        got = flip(x, "dp", mask)
        if mask == 1:
            got = after(got, fillers[0](x))
        x = ordered(x, got, is_upper("dp", mask), spot)
    upper = side != 0
    low, high = x[..., :channels], x[..., channels:]
    outer = jnp.where(upper, high, low)
    other = after(flip(outer, "x", 1), fillers[1](outer))
    x = jnp.concatenate(
        [jnp.where(upper, other, low), jnp.where(upper, low, high), jnp.where(upper, high, other)],
        axis=-1,
    )
    x = ordered(x, flip(x, "core"), is_upper("core", 1), x.ndim - 2)
    return x.reshape(share * lax.axis_size("dp"), wide)


class Chain:
    def __init__(self, keep, *sends):
        shards, taps, half, cols = keep.shape
        dp_masks = bits_of(shards)[::-1]
        x_masks = bits_of(lax.axis_size("x"))[::-1]
        nd, nx = len(dp_masks), len(x_masks)
        shape = (2,) * (nd + nx) + (taps >> nx, half, cols)
        gots = [flip(send, "core") for send in sends]
        if len(gots) == 1:
            self.got, self.pair = gots[0].reshape(shape), None
        else:
            shape_of_one = shape[:nd] + (1,) + shape[nd + 1 :]
            self.got, self.pair = (got.reshape(shape_of_one) for got in gots)
        self.keep = keep.reshape(shape)
        self.stages = [("x", m, nd + i) for i, m in enumerate(x_masks)]
        self.stages += [("dp", m, i) for i, m in list(enumerate(dp_masks))[::-1]]

    def launch(self, *tokens):
        if tokens:
            self.got = after(self.got, *tokens)
        axis, mask, spot = self.stages.pop(0)
        bit = is_upper(axis, mask).astype(jnp.int32)

        def pick(which):
            kept = lax.dynamic_index_in_dim(self.keep, which, spot)
            if self.pair is not None:
                return kept + jnp.where(which != 0, self.pair, self.got).astype(f32)
            return kept + lax.dynamic_index_in_dim(self.got, which, spot).astype(f32)

        other = pick(1 - bit).astype(bf16)
        self.keep, self.got, self.pair = pick(bit), flip(other, axis, mask), None
        return other

    def land(self, token):
        self.keep, self.got = lax.optimization_barrier((self.keep, self.got, token))[:2]

    def finish(self):
        while self.stages:
            self.launch()
        x = self.keep + self.got.astype(f32)
        return x.reshape(x.shape[-3:])


def join_x(x, token=None):
    for mask in bits_of(lax.axis_size("x")):
        got = flip(x, "x", mask)
        if token is not None:
            x, got = lax.optimization_barrier((x, got, token))[:2]
        x = ordered(x, got, is_upper("x", mask), 1)
    return x


def join_core(x):
    return ordered(x, flip(x, "core"), is_upper("core", 1), 2)


def matmul_nt(a, b):
    return lax.dot_general(a, b, (((1,), (1,)), ((), ())), preferred_element_type=f32)


def matmul_tn(a, b):
    return lax.dot_general(a, b, (((0,), (0,)), ((), ())), preferred_element_type=f32)


def matmul(a, b):
    return jnp.dot(a, b, preferred_element_type=f32)


def group_mean(sums, same_ref, count):
    filled = -(-len(sums) // 8) * 8
    padded = jnp.concatenate(sums + [sums[0]] * (filled - len(sums)), axis=0)
    total = jnp.dot(
        padded, same_ref[...], precision=lax.Precision.HIGHEST, preferred_element_type=f32
    )
    return total * (1.0 / count)


def write_views(ref, frame, values, breadth):
    pixels, channels = values.shape
    height = pixels // breadth
    column = lax.broadcasted_iota(jnp.int32, (pixels, channels), 0) & (breadth - 1)
    left = jnp.where(column == 0, 0.0, pltpu.roll(values, 1, 0))
    right = jnp.where(column == breadth - 1, 0.0, pltpu.roll(values, pixels - 1, 0))
    edge = jnp.zeros((1, breadth, 3 * channels), bf16)
    ref[frame, 0:1] = edge
    ref[frame, height + 1 : height + 2] = edge
    for s, moved in enumerate((left, values, right)):
        ref[frame, 1 : height + 1, :, s * channels : (s + 1) * channels] = moved.astype(
            bf16
        ).reshape(height, breadth, channels)


def rows_of(views_ref, r):
    frames, high, breadth, wide = views_ref.shape
    return views_ref[:, pl.ds(r, high - 2)].reshape(frames * (high - 2) * breadth, wide)


def norm_kernel(count, breadth, x_ref, same_ref, views_ref, mean_ref, scale_ref):
    frames = range(x_ref.shape[0])
    sums = [jnp.sum(x_ref[f].astype(f32), axis=0, keepdims=True) for f in frames]
    centers = group_mean(sums, same_ref, count)
    squares = []
    for f in frames:
        deviation = x_ref[f].astype(f32) - centers[f : f + 1]
        squares.append(jnp.sum(deviation * deviation, axis=0, keepdims=True))
    scales = lax.rsqrt(group_mean(squares, same_ref, count) + epsilon)
    for f in frames:
        center, scaled = centers[f : f + 1], scales[f : f + 1]
        normal = (x_ref[f].astype(f32) - center) * scaled
        mean_ref[f] = center
        scale_ref[f] = scaled
        write_views(views_ref, f, normal / (1.0 + jnp.exp(-normal)), breadth)


def normalize(frames, same, breadth):
    count, pixels, channels = frames.shape
    height = pixels // breadth
    return pl.pallas_call(
        lambda *refs: norm_kernel(pixels * (channels // GROUPS), breadth, *refs),
        out_shape=(
            jax.ShapeDtypeStruct((count, height + 2, breadth, 3 * channels), bf16),
            jax.ShapeDtypeStruct((count, 1, channels), f32),
            jax.ShapeDtypeStruct((count, 1, channels), f32),
        ),
        compiler_params=params(),
        cost_estimate=cost(7.6),
        name="norm",
    )(frames, same)


def turn_kernel(views_ref, out_ref):
    out_ref[0] = rows_of(views_ref, pl.program_id(0)).T


def turned_columns(views):
    frames, high, breadth, wide = views.shape
    rows = frames * (high - 2) * breadth
    return pl.pallas_call(
        turn_kernel,
        grid=(3,),
        in_specs=[whole(views.shape)],
        out_specs=pl.BlockSpec((1, wide, rows), lambda i: (i, 0, 0)),
        out_shape=jax.ShapeDtypeStruct((3, wide, rows), bf16),
        compiler_params=params(),
        cost_estimate=cost(8.5),
        name="turn",
    )(views)


def hidden_grad_kernel(breadth, cot_ref, next_ref, w_ref, back_ref, views_ref, sum_ref):
    outs = cot_ref.shape[0]
    channels = w_ref.shape[0]
    total = jnp.zeros((1, channels), f32)
    for o in range(outs):
        later = cot_ref[o + 1] if o + 1 < outs else next_ref[...]
        even = matmul_nt(cot_ref[o], w_ref[:, channels : 2 * channels])
        odd = matmul_nt(cot_ref[o], w_ref[:, 2 * channels : 3 * channels]) + matmul_nt(
            later, w_ref[:, :channels]
        )
        for frame, values in ((2 * o, even), (2 * o + 1, odd)):
            back_ref[frame] = values.astype(bf16)
            write_views(views_ref, frame, values, breadth)
            total += jnp.sum(values, axis=0, keepdims=True)
    sum_ref[...] = total


def hidden_gradient(cot, following, temporal, breadth):
    outs, pixels, channels = cot.shape
    return pl.pallas_call(
        lambda *refs: hidden_grad_kernel(breadth, *refs),
        out_shape=(
            jax.ShapeDtypeStruct((2 * outs, pixels, channels), bf16),
            jax.ShapeDtypeStruct((2 * outs, pixels // breadth + 2, breadth, 3 * channels), bf16),
            jax.ShapeDtypeStruct((1, channels), f32),
        ),
        compiler_params=params(VMEM_BYTES // 2),
        cost_estimate=cost(6.5),
        name="hidden_grad",
    )(cot, following, temporal)


def store_halves(core_ref, grad, keep_ref, send_ref, slot, send_slot):
    shards, _, half, channels = keep_ref.shape
    grad = grad.reshape(shards, 2 * half, channels)
    low, high = grad[:, :half], grad[:, half:]

    @pl.when(core_ref[0] == 0)
    def _():
        keep_ref[:, slot] = low
        send_ref[:, send_slot] = high.astype(bf16)

    @pl.when(core_ref[0] != 0)
    def _():
        keep_ref[:, slot] = high
        send_ref[:, send_slot] = low.astype(bf16)


def weight_grad_kernel(core_ref, x_ref, back_ref, keep_ref, send_ref):
    both = x_ref[...]
    grads = matmul(both.reshape(both.shape[0] * both.shape[1], both.shape[2]), back_ref[...])
    for k in range(2):
        grad = grads[k * both.shape[1] : (k + 1) * both.shape[1]]
        store_halves(core_ref, grad, keep_ref, send_ref, k, k)


def weight_grad(turned, hidden_back, first, shards, core):
    rows, channels = hidden_back.shape
    half = channels // shards // 2
    out_spec = pl.BlockSpec((shards, 2, half, channels), lambda i: (0, i, 0, 0))
    return pl.pallas_call(
        weight_grad_kernel,
        grid=(2,),
        in_specs=[
            pl.BlockSpec(memory_space=pltpu.SMEM),
            pl.BlockSpec((2, channels, rows), lambda i: (first // 2 + i, 0, 0)),
            whole((rows, channels)),
        ],
        out_specs=(out_spec, out_spec),
        out_shape=(
            jax.ShapeDtypeStruct((shards, 4, half, channels), f32),
            jax.ShapeDtypeStruct((shards, 4, half, channels), bf16),
        ),
        compiler_params=params(),
        cost_estimate=cost(8.5),
        name="weight_grad",
    )(core, turned, hidden_back)


def last_grad_kernel(
    core_ref, x_ref, back_ref, hidden_ref, before_ref, cot_ref, keep_ref, one_ref, two_ref
):
    sends = ((one_ref, 0), (one_ref, 1), (two_ref, 0), (two_ref, 1))
    grad = matmul(x_ref[0], back_ref[...])
    store_halves(core_ref, grad, keep_ref, sends[0][0], 0, sends[0][1])
    outs, pixels, channels = cot_ref.shape
    seen = []
    for o in range(outs):
        first = before_ref[...] if o == 0 else hidden_ref[2 * o - 1]
        seen.append(jnp.concatenate([first, hidden_ref[2 * o], hidden_ref[2 * o + 1]], axis=1))
    grads = matmul_tn(
        jnp.concatenate(seen, axis=0), cot_ref[...].reshape(outs * pixels, channels)
    )
    for k in range(3):
        grad = grads[k * channels : (k + 1) * channels]
        store_halves(core_ref, grad, keep_ref, sends[1 + k][0], 1 + k, sends[1 + k][1])


def last_grad(turned, hidden_back, hidden, before, cot, shards, core):
    rows, channels = hidden_back.shape
    half = channels // shards // 2
    shape = (shards, 4, half, channels)
    two = (shards, 2, half, channels)
    return pl.pallas_call(
        last_grad_kernel,
        grid=(1,),
        in_specs=[
            pl.BlockSpec(memory_space=pltpu.SMEM),
            pl.BlockSpec((1, channels, rows), lambda i: (8, 0, 0)),
            whole((rows, channels)),
            whole(hidden.shape),
            whole(before.shape),
            whole(cot.shape),
        ],
        out_specs=(whole(shape), whole(two), whole(two)),
        out_shape=(
            jax.ShapeDtypeStruct(shape, f32),
            jax.ShapeDtypeStruct(two, bf16),
            jax.ShapeDtypeStruct(two, bf16),
        ),
        compiler_params=params(),
        cost_estimate=cost(10.3),
        name="last_grad",
    )(core, turned, hidden_back, hidden, before, cot)


def temporal_kernel(hidden_ref, before_ref, w_ref, out_ref):
    channels = w_ref.shape[0]
    for o in range(out_ref.shape[0]):
        total = 0.0
        for k in range(3):
            frame = 2 * o + k - 1
            x = before_ref[...] if frame < 0 else hidden_ref[frame]
            total += matmul(x, w_ref[:, k * channels : (k + 1) * channels])
        out_ref[o] = total


def temporal_forward(hidden, before, temporal):
    frames, pixels, channels = hidden.shape
    return pl.pallas_call(
        temporal_kernel,
        out_shape=jax.ShapeDtypeStruct((frames // 2, pixels, channels), f32),
        compiler_params=params(),
        cost_estimate=cost(5.2),
        name="temporal",
    )(hidden, before, temporal)


def conv_forward_kernel(views_ref, w_ref, shift_ref, out_ref, last_ref, acc_ref, tall_ref):
    r = pl.program_id(0)
    rows, channels = acc_ref.shape
    for s in range(3):
        tall_ref[s * channels : (s + 1) * channels] = w_ref[:, s * channels : (s + 1) * channels]
    part = matmul(rows_of(views_ref, r), tall_ref[...])

    @pl.when(r == 0)
    def _():
        acc_ref[...] = part + shift_ref[...]

    @pl.when(r == 1)
    def _():
        acc_ref[...] += part

    @pl.when(r == 2)
    def _():
        hidden = (acc_ref[...] + part).astype(bf16).reshape(out_ref.shape)
        out_ref[...] = hidden
        last_ref[...] = hidden[-1]


def conv_forward(views, spatial, shift):
    frames, high, breadth, wide = views.shape
    channels = wide // 3
    pixels = (high - 2) * breadth
    return pl.pallas_call(
        conv_forward_kernel,
        grid=(3,),
        in_specs=[
            whole(views.shape),
            pl.BlockSpec((channels, wide), lambda i: (0, i)),
            whole((1, channels)),
        ],
        out_specs=(whole((frames, pixels, channels)), whole((pixels, channels))),
        out_shape=(
            jax.ShapeDtypeStruct((frames, pixels, channels), bf16),
            jax.ShapeDtypeStruct((pixels, channels), bf16),
        ),
        scratch_shapes=[
            pltpu.VMEM((frames * pixels, channels), f32),
            pltpu.VMEM((wide, channels), bf16),
        ],
        compiler_params=params(),
        cost_estimate=cost(15),
        name="conv_forward",
    )(views, spatial, shift)


def back_part(views_ref, w_ref, r):
    channels = w_ref.shape[0]
    x = rows_of(views_ref, 2 - r)
    x = jnp.concatenate(
        [x[:, (2 - s) * channels : (3 - s) * channels] for s in range(3)], axis=1
    )
    return matmul_nt(x, w_ref[...])


def conv_back_kernel(views_ref, w_ref, acc_ref):
    r = pl.program_id(0)
    part = back_part(views_ref, w_ref, r)

    @pl.when(r == 0)
    def _():
        acc_ref[...] = part

    @pl.when(r != 0)
    def _():
        acc_ref[...] += part


def conv_back_start(views, spatial):
    frames, high, breadth, wide = views.shape
    channels = wide // 3
    rows = frames * (high - 2) * breadth
    return pl.pallas_call(
        conv_back_kernel,
        grid=(2,),
        in_specs=[whole(views.shape), pl.BlockSpec((channels, wide), lambda i: (0, i))],
        out_specs=whole((rows, channels)),
        out_shape=jax.ShapeDtypeStruct((rows, channels), f32),
        compiler_params=params(),
        cost_estimate=cost(12),
        name="conv_back_start",
    )(views, spatial)


def conv_back_end_kernel(
    count, views_ref, w_ref, part_ref, x_ref, mean_ref, scale_ref, same_ref, out_ref, acc_ref
):
    acc_ref[...] = part_ref[...] + back_part(views_ref, w_ref, 2)
    back_through_norm(count, x_ref, mean_ref, scale_ref, same_ref, out_ref, acc_ref)


def back_through_norm(count, x_ref, mean_ref, scale_ref, same_ref, out_ref, acc_ref):
    frames, pixels, _ = x_ref.shape

    def parts(f):
        normal = (x_ref[f].astype(f32) - mean_ref[f]) * scale_ref[f]
        gate = 1.0 / (1.0 + jnp.exp(-normal))
        slope = gate * (1.0 + normal * (1.0 - gate))
        return normal, slope

    sums = []
    for f in range(frames):
        normal, slope = parts(f)
        grad = acc_ref[f * pixels : (f + 1) * pixels] * slope
        acc_ref[f * pixels : (f + 1) * pixels] = grad
        sums.append(jnp.sum(grad, axis=0, keepdims=True))
        sums.append(jnp.sum(grad * normal, axis=0, keepdims=True))
    means = group_mean(sums, same_ref, count)
    for f in range(frames):
        normal = (x_ref[f].astype(f32) - mean_ref[f]) * scale_ref[f]
        one, two = means[2 * f : 2 * f + 1], means[2 * f + 1 : 2 * f + 2]
        grad = acc_ref[f * pixels : (f + 1) * pixels]
        out_ref[f] = (grad - one - normal * two) * scale_ref[f]


def conv_back_end(views, spatial, part, frames, mean, scale, same):
    count, pixels, channels = frames.shape
    return pl.pallas_call(
        lambda *refs: conv_back_end_kernel(pixels * (channels // GROUPS), *refs),
        grid=(1,),
        in_specs=[
            whole(views.shape),
            pl.BlockSpec((channels, 3 * channels), lambda i: (0, 2)),
            whole(part.shape),
            whole(frames.shape),
            whole(mean.shape),
            whole(scale.shape),
            whole(same.shape),
        ],
        out_specs=whole(frames.shape),
        out_shape=jax.ShapeDtypeStruct(frames.shape, f32),
        scratch_shapes=[pltpu.VMEM((count * pixels, channels), f32)],
        compiler_params=params(),
        cost_estimate=cost(12),
        name="conv_back_end",
    )(views, spatial, part, frames, mean, scale, same)


def neighbours(x_size, step):
    count = 2 * x_size
    return [(i, i + step) for i in range(count) if 0 <= i + step < count]


def body(latents, cotangent, timesteps, spatial_weight, temporal_weight, time_weight):
    clip_frames = latents[0]
    frame_count, height, breadth, channels = clip_frames.shape
    pixels = height * breadth
    out_count = frame_count // 2
    dp = lax.axis_size("dp")
    x_size = lax.axis_size("x")
    share = channels // dp
    half = share // 2
    core = lax.axis_index("core")
    core_scalar = core[None].astype(jnp.int32)
    frames = clip_frames.reshape(frame_count, pixels, channels)

    cot = cotangent[0].reshape(out_count, pixels, channels)
    following = lax.ppermute(cot[0], ("x", "core"), neighbours(x_size, -1))

    spatial = jnp.concatenate([spatial_weight, time_weight], axis=1)
    spatial_mine = lax.dynamic_slice_in_dim(spatial, core * half, half, axis=0)
    spatial_full = lax.all_gather(spatial_mine, ("dp", "core"), axis=0, tiled=True)
    group = lax.broadcasted_iota(jnp.int32, (channels, channels), 0) // (channels // GROUPS)
    same = (group == group.T).astype(f32)
    held = {}

    def activate(token):
        held["views"], held["mean"], held["scale"] = normalize(
            after(frames, token), same, breadth
        )
        return held["mean"]

    def turn(token):
        held["turned"] = turned_columns(after(held["views"], token))
        return held["turned"]

    temporal_full = gather_temporal(temporal_weight, (activate, turn))
    views, mean, scale = held["views"], held["mean"], held["scale"]
    turned = held["turned"].reshape(9, channels, frame_count * pixels)

    embedded = embedding(timesteps[0], time_weight.shape[1])
    hidden_back, back_views, shift_sum = hidden_gradient(cot, following, temporal_full, breadth)
    flat_back = hidden_back.reshape(frame_count * pixels, channels)
    pairs = jnp.concatenate([shift_sum, embedded[None]], axis=1)
    pairs = jnp.pad(pairs, ((0, 0), (0, PAIR_WIDTH - pairs.shape[1])))
    pairs = lax.all_gather(pairs, ("dp", "x", "core"), axis=0, tiled=True)

    one = weight_grad(turned, flat_back, 0, dp, core_scalar)
    chain_a = Chain(*one)
    two = weight_grad(turned, flat_back, 4, dp, core_scalar)
    chain_a.land(two[1])
    chain_b = Chain(*two)
    out_a = chain_a.launch()

    time_full = spatial_full[:, 9 * channels :]
    time_shift = jnp.dot(time_full.astype(f32), embedded, precision=lax.Precision.HIGHEST)
    hidden, end = conv_forward(views, spatial_full, after(time_shift, out_a)[None])
    chain_a.land(hidden)
    chain_b.land(hidden)
    before = lax.ppermute(end, ("x", "core"), neighbours(x_size, 1))
    out_a = chain_a.launch()
    out_b = chain_b.launch(before)
    last = last_grad(turned, flat_back, after(hidden, out_a, out_b), before, cot, dp, core_scalar)
    chain_a.land(last[1])
    chain_b.land(last[1])
    chain_c = Chain(*last)
    out_a = chain_a.launch()
    out_b = chain_b.launch(out_a)
    out_c = chain_c.launch(out_b)

    part = conv_back_start(after(back_views, out_c), spatial_full)
    chain_a.land(part)
    chain_b.land(part)
    chain_c.land(part)
    out_a = chain_a.launch()
    out_b = chain_b.launch(out_a)
    out_c = chain_c.launch(out_b)
    input_grad = conv_back_end(
        after(back_views, out_c), spatial_full, part, frames, mean, scale, same
    )
    chain_a.land(input_grad)
    chain_b.land(input_grad)
    chain_c.land(input_grad)
    out_c = chain_c.launch()
    first = chain_a.finish()
    out_b = chain_b.launch(out_c)

    downsampled = temporal_forward(after(hidden, first, out_b), before, temporal_full)
    chain_b.land(downsampled)
    chain_c.land(downsampled)
    rows = jnp.stack([first, chain_b.finish()])
    out_c = chain_c.launch(rows)
    rows = join_x(rows)
    last_rows = join_core(join_x(chain_c.finish()[None]))[0]
    rows = join_core(rows)
    downsampled = downsampled.reshape(1, out_count, height, breadth, channels)
    input_grad = input_grad.reshape(1, frame_count, height, breadth, channels)

    mine = lax.dynamic_slice_in_dim(
        pairs[:, :channels], lax.axis_index("dp") * share, share, axis=1
    )
    time_grad = lax.dot_general(
        mine,
        pairs[:, channels : channels + time_weight.shape[1]],
        (((0,), (0,)), ((), ())),
        precision=lax.Precision.HIGHEST,
        preferred_element_type=f32,
    )

    spatial_grad = jnp.concatenate(
        [rows[i, j] for i in range(2) for j in range(4)] + [last_rows[0]], axis=1
    )
    temporal_grad = jnp.concatenate([last_rows[1 + k] for k in range(3)], axis=1)
    return (downsampled, input_grad, spatial_grad, temporal_grad, time_grad)


def solution(mesh):
    dp, tm = mesh.devices.shape
    fine = Mesh(mesh.devices.reshape(dp, tm // 2, 2), ("dp", "x", "core"))
    placed = (
        P("dp", ("x", "core"), None, None, None),
        P("dp", ("x", "core"), None, None, None),
        P("dp"),
        P("dp", None),
        P("dp", None),
        P("dp", None),
    )
    return jax.shard_map(
        body,
        mesh=fine,
        in_specs=placed,
        out_specs=(
            P("dp", ("x", "core"), None, None, None),
            P("dp", ("x", "core"), None, None, None),
            P("dp", None),
            P("dp", None),
            P("dp", None),
        ),
        check_vma=False,
    )
```

```python
import math

import jax
import jax.numpy as jnp
from jax import lax
from jax.experimental import pallas as pl
from jax.experimental.pallas import tpu as pltpu
from jax.sharding import Mesh
from jax.sharding import PartitionSpec as P

GROUPS = 32


epsilon = 1e-05
log_base = math.log(10000.0)
bf16 = jnp.bfloat16
f32 = jnp.float32
VMEM_BYTES = 56 * 1024 * 1024
PAIR_WIDTH = 8960


def embedding(diffusion_step, embed_width):
    half_width = embed_width // 2
    frequency = jnp.exp(-log_base * jnp.arange(half_width, dtype=jnp.float32) / half_width)
    angles = diffusion_step.astype(jnp.float32) * frequency
    return jnp.concatenate([jnp.cos(angles), jnp.sin(angles)])


def flip(x, axis, mask=1):
    count = lax.axis_size(axis)
    return lax.ppermute(x, axis, [(i, i ^ mask) for i in range(count)])


def bits_of(count):
    return [1 << i for i in range(count.bit_length() - 1)]


def params(size=VMEM_BYTES):
    return pltpu.CompilerParams(vmem_limit_bytes=size)


def cost(microseconds):
    return pl.CostEstimate(
        flops=int(microseconds * 1.15e9), transcendentals=0, bytes_accessed=int(microseconds * 1e5)
    )


def whole(shape):
    return pl.BlockSpec(shape, lambda *_: (0,) * len(shape), pipeline_mode=pl.Buffered(1))


def is_upper(axis, mask):
    return (lax.axis_index(axis) & mask) != 0


def after(x, *others):
    return lax.optimization_barrier((x,) + others)[0]


def ordered(mine, other, upper, axis):
    low = jnp.where(upper, other, mine)
    high = jnp.where(upper, mine, other)
    return jnp.concatenate([low, high], axis=axis)


def gather_temporal(weight, fillers):
    share, wide = weight.shape
    channels = wide // 3
    half = share // 2
    side = lax.axis_index("x") & 1
    x = lax.dynamic_slice(
        weight, (lax.axis_index("core") * half, side * channels), (half, 2 * channels)
    )
    masks = bits_of(lax.axis_size("dp"))[::-1]
    x = x.reshape((1,) * len(masks) + x.shape)
    for spot, mask in enumerate(masks):
        got = flip(x, "dp", mask)
        if mask == 1:
            got = after(got, fillers[0](x))
        x = ordered(x, got, is_upper("dp", mask), spot)
    upper = side != 0
    low, high = x[..., :channels], x[..., channels:]
    outer = jnp.where(upper, high, low)
    other = after(flip(outer, "x", 1), fillers[1](outer))
    x = jnp.concatenate(
        [jnp.where(upper, other, low), jnp.where(upper, low, high), jnp.where(upper, high, other)],
        axis=-1,
    )
    x = ordered(x, flip(x, "core"), is_upper("core", 1), x.ndim - 2)
    return x.reshape(share * lax.axis_size("dp"), wide)


class Chain:
    def __init__(self, keep, *sends):
        shards, taps, half, cols = keep.shape
        dp_masks = bits_of(shards)[::-1]
        x_masks = bits_of(lax.axis_size("x"))[::-1]
        nd, nx = len(dp_masks), len(x_masks)
        shape = (2,) * (nd + nx) + (taps >> nx, half, cols)
        gots = [flip(send, "core") for send in sends]
        if len(gots) == 1:
            self.got, self.pair = gots[0].reshape(shape), None
        else:
            shape_of_one = shape[:nd] + (1,) + shape[nd + 1 :]
            self.got, self.pair = (got.reshape(shape_of_one) for got in gots)
        self.keep = keep.reshape(shape)
        self.stages = [("x", m, nd + i) for i, m in enumerate(x_masks)]
        self.stages += [("dp", m, i) for i, m in list(enumerate(dp_masks))[::-1]]

    def launch(self, *tokens):
        if tokens:
            self.got = after(self.got, *tokens)
        axis, mask, spot = self.stages.pop(0)
        bit = is_upper(axis, mask).astype(jnp.int32)

        def pick(which):
            kept = lax.dynamic_index_in_dim(self.keep, which, spot)
            if self.pair is not None:
                return kept + jnp.where(which != 0, self.pair, self.got).astype(f32)
            return kept + lax.dynamic_index_in_dim(self.got, which, spot).astype(f32)

        other = pick(1 - bit).astype(bf16)
        self.keep, self.got, self.pair = pick(bit), flip(other, axis, mask), None
        return other

    def land(self, token):
        self.keep, self.got = lax.optimization_barrier((self.keep, self.got, token))[:2]

    def finish(self):
        while self.stages:
            self.launch()
        x = self.keep + self.got.astype(f32)
        return x.reshape(x.shape[-3:])


def join_x(x, token=None):
    for mask in bits_of(lax.axis_size("x")):
        got = flip(x, "x", mask)
        if token is not None:
            x, got = lax.optimization_barrier((x, got, token))[:2]
        x = ordered(x, got, is_upper("x", mask), 1)
    return x


def join_core(x):
    return ordered(x, flip(x, "core"), is_upper("core", 1), 2)


def matmul_nt(a, b):
    return lax.dot_general(a, b, (((1,), (1,)), ((), ())), preferred_element_type=f32)


def matmul_tn(a, b):
    return lax.dot_general(a, b, (((0,), (0,)), ((), ())), preferred_element_type=f32)


def matmul(a, b):
    return jnp.dot(a, b, preferred_element_type=f32)


def group_mean(sums, same_ref, count):
    filled = -(-len(sums) // 8) * 8
    padded = jnp.concatenate(sums + [sums[0]] * (filled - len(sums)), axis=0)
    total = jnp.dot(
        padded, same_ref[...], precision=lax.Precision.HIGHEST, preferred_element_type=f32
    )
    return total * (1.0 / count)


def write_views(ref, frame, values, breadth):
    pixels, channels = values.shape
    height = pixels // breadth
    column = lax.broadcasted_iota(jnp.int32, (pixels, channels), 0) & (breadth - 1)
    left = jnp.where(column == 0, 0.0, pltpu.roll(values, 1, 0))
    right = jnp.where(column == breadth - 1, 0.0, pltpu.roll(values, pixels - 1, 0))
    edge = jnp.zeros((1, breadth, 3 * channels), bf16)
    ref[frame, 0:1] = edge
    ref[frame, height + 1 : height + 2] = edge
    for s, moved in enumerate((left, values, right)):
        ref[frame, 1 : height + 1, :, s * channels : (s + 1) * channels] = moved.astype(
            bf16
        ).reshape(height, breadth, channels)


def rows_of(views_ref, r):
    frames, high, breadth, wide = views_ref.shape
    return views_ref[:, pl.ds(r, high - 2)].reshape(frames * (high - 2) * breadth, wide)


def norm_kernel(count, breadth, x_ref, same_ref, views_ref, mean_ref, scale_ref):
    frames = range(x_ref.shape[0])
    sums = [jnp.sum(x_ref[f].astype(f32), axis=0, keepdims=True) for f in frames]
    centers = group_mean(sums, same_ref, count)
    squares = []
    for f in frames:
        deviation = x_ref[f].astype(f32) - centers[f : f + 1]
        squares.append(jnp.sum(deviation * deviation, axis=0, keepdims=True))
    scales = lax.rsqrt(group_mean(squares, same_ref, count) + epsilon)
    for f in frames:
        center, scaled = centers[f : f + 1], scales[f : f + 1]
        normal = (x_ref[f].astype(f32) - center) * scaled
        mean_ref[f] = center
        scale_ref[f] = scaled
        write_views(views_ref, f, normal / (1.0 + jnp.exp(-normal)), breadth)


def normalize(frames, same, breadth):
    count, pixels, channels = frames.shape
    height = pixels // breadth
    return pl.pallas_call(
        lambda *refs: norm_kernel(pixels * (channels // GROUPS), breadth, *refs),
        out_shape=(
            jax.ShapeDtypeStruct((count, height + 2, breadth, 3 * channels), bf16),
            jax.ShapeDtypeStruct((count, 1, channels), f32),
            jax.ShapeDtypeStruct((count, 1, channels), f32),
        ),
        compiler_params=params(),
        cost_estimate=cost(7.6),
        name="norm",
    )(frames, same)


def turn_kernel(views_ref, out_ref):
    out_ref[0] = rows_of(views_ref, pl.program_id(0)).T


def turned_columns(views):
    frames, high, breadth, wide = views.shape
    rows = frames * (high - 2) * breadth
    return pl.pallas_call(
        turn_kernel,
        grid=(3,),
        in_specs=[whole(views.shape)],
        out_specs=pl.BlockSpec((1, wide, rows), lambda i: (i, 0, 0)),
        out_shape=jax.ShapeDtypeStruct((3, wide, rows), bf16),
        compiler_params=params(),
        cost_estimate=cost(8.5),
        name="turn",
    )(views)


def hidden_grad_kernel(breadth, cot_ref, next_ref, w_ref, back_ref, views_ref, sum_ref):
    outs = cot_ref.shape[0]
    channels = w_ref.shape[0]
    total = jnp.zeros((1, channels), f32)
    for o in range(outs):
        later = cot_ref[o + 1] if o + 1 < outs else next_ref[...]
        even = matmul_nt(cot_ref[o], w_ref[:, channels : 2 * channels])
        odd = matmul_nt(cot_ref[o], w_ref[:, 2 * channels : 3 * channels]) + matmul_nt(
            later, w_ref[:, :channels]
        )
        for frame, values in ((2 * o, even), (2 * o + 1, odd)):
            back_ref[frame] = values.astype(bf16)
            write_views(views_ref, frame, values, breadth)
            total += jnp.sum(values, axis=0, keepdims=True)
    sum_ref[...] = total


def hidden_gradient(cot, following, temporal, breadth):
    outs, pixels, channels = cot.shape
    return pl.pallas_call(
        lambda *refs: hidden_grad_kernel(breadth, *refs),
        out_shape=(
            jax.ShapeDtypeStruct((2 * outs, pixels, channels), bf16),
            jax.ShapeDtypeStruct((2 * outs, pixels // breadth + 2, breadth, 3 * channels), bf16),
            jax.ShapeDtypeStruct((1, channels), f32),
        ),
        compiler_params=params(VMEM_BYTES // 2),
        cost_estimate=cost(6.5),
        name="hidden_grad",
    )(cot, following, temporal)


def store_halves(core_ref, grad, keep_ref, send_ref, slot, send_slot):
    shards, _, half, channels = keep_ref.shape
    grad = grad.reshape(shards, 2 * half, channels)
    low, high = grad[:, :half], grad[:, half:]

    @pl.when(core_ref[0] == 0)
    def _():
        keep_ref[:, slot] = low
        send_ref[:, send_slot] = high.astype(bf16)

    @pl.when(core_ref[0] != 0)
    def _():
        keep_ref[:, slot] = high
        send_ref[:, send_slot] = low.astype(bf16)


def weight_grad_kernel(core_ref, x_ref, back_ref, keep_ref, send_ref):
    both = x_ref[...]
    grads = matmul(both.reshape(both.shape[0] * both.shape[1], both.shape[2]), back_ref[...])
    for k in range(2):
        grad = grads[k * both.shape[1] : (k + 1) * both.shape[1]]
        store_halves(core_ref, grad, keep_ref, send_ref, k, k)


def weight_grad(turned, hidden_back, first, shards, core):
    rows, channels = hidden_back.shape
    half = channels // shards // 2
    out_spec = pl.BlockSpec((shards, 2, half, channels), lambda i: (0, i, 0, 0))
    return pl.pallas_call(
        weight_grad_kernel,
        grid=(2,),
        in_specs=[
            pl.BlockSpec(memory_space=pltpu.SMEM),
            pl.BlockSpec((2, channels, rows), lambda i: (first // 2 + i, 0, 0)),
            whole((rows, channels)),
        ],
        out_specs=(out_spec, out_spec),
        out_shape=(
            jax.ShapeDtypeStruct((shards, 4, half, channels), f32),
            jax.ShapeDtypeStruct((shards, 4, half, channels), bf16),
        ),
        compiler_params=params(),
        cost_estimate=cost(8.5),
        name="weight_grad",
    )(core, turned, hidden_back)


def last_grad_kernel(
    core_ref, x_ref, back_ref, hidden_ref, before_ref, cot_ref, keep_ref, one_ref, two_ref
):
    sends = ((one_ref, 0), (one_ref, 1), (two_ref, 0), (two_ref, 1))
    grad = matmul(x_ref[0], back_ref[...])
    store_halves(core_ref, grad, keep_ref, sends[0][0], 0, sends[0][1])
    outs, pixels, channels = cot_ref.shape
    seen = []
    for o in range(outs):
        first = before_ref[...] if o == 0 else hidden_ref[2 * o - 1]
        seen.append(jnp.concatenate([first, hidden_ref[2 * o], hidden_ref[2 * o + 1]], axis=1))
    grads = matmul_tn(
        jnp.concatenate(seen, axis=0), cot_ref[...].reshape(outs * pixels, channels)
    )
    for k in range(3):
        grad = grads[k * channels : (k + 1) * channels]
        store_halves(core_ref, grad, keep_ref, sends[1 + k][0], 1 + k, sends[1 + k][1])


def last_grad(turned, hidden_back, hidden, before, cot, shards, core):
    rows, channels = hidden_back.shape
    half = channels // shards // 2
    shape = (shards, 4, half, channels)
    two = (shards, 2, half, channels)
    return pl.pallas_call(
        last_grad_kernel,
        grid=(1,),
        in_specs=[
            pl.BlockSpec(memory_space=pltpu.SMEM),
            pl.BlockSpec((1, channels, rows), lambda i: (8, 0, 0)),
            whole((rows, channels)),
            whole(hidden.shape),
            whole(before.shape),
            whole(cot.shape),
        ],
        out_specs=(whole(shape), whole(two), whole(two)),
        out_shape=(
            jax.ShapeDtypeStruct(shape, f32),
            jax.ShapeDtypeStruct(two, bf16),
            jax.ShapeDtypeStruct(two, bf16),
        ),
        compiler_params=params(),
        cost_estimate=cost(10.3),
        name="last_grad",
    )(core, turned, hidden_back, hidden, before, cot)


def temporal_kernel(hidden_ref, before_ref, w_ref, out_ref):
    channels = w_ref.shape[0]
    for o in range(out_ref.shape[0]):
        total = 0.0
        for k in range(3):
            frame = 2 * o + k - 1
            x = before_ref[...] if frame < 0 else hidden_ref[frame]
            total += matmul(x, w_ref[:, k * channels : (k + 1) * channels])
        out_ref[o] = total


def temporal_forward(hidden, before, temporal):
    frames, pixels, channels = hidden.shape
    return pl.pallas_call(
        temporal_kernel,
        out_shape=jax.ShapeDtypeStruct((frames // 2, pixels, channels), f32),
        compiler_params=params(),
        cost_estimate=cost(5.2),
        name="temporal",
    )(hidden, before, temporal)


def conv_forward_kernel(views_ref, w_ref, shift_ref, out_ref, last_ref, acc_ref, tall_ref):
    r = pl.program_id(0)
    rows, channels = acc_ref.shape
    for s in range(3):
        tall_ref[s * channels : (s + 1) * channels] = w_ref[:, s * channels : (s + 1) * channels]
    part = matmul(rows_of(views_ref, r), tall_ref[...])

    @pl.when(r == 0)
    def _():
        acc_ref[...] = part + shift_ref[...]

    @pl.when(r == 1)
    def _():
        acc_ref[...] += part

    @pl.when(r == 2)
    def _():
        hidden = (acc_ref[...] + part).astype(bf16).reshape(out_ref.shape)
        out_ref[...] = hidden
        last_ref[...] = hidden[-1]


def conv_forward(views, spatial, shift):
    frames, high, breadth, wide = views.shape
    channels = wide // 3
    pixels = (high - 2) * breadth
    return pl.pallas_call(
        conv_forward_kernel,
        grid=(3,),
        in_specs=[
            whole(views.shape),
            pl.BlockSpec((channels, wide), lambda i: (0, i)),
            whole((1, channels)),
        ],
        out_specs=(whole((frames, pixels, channels)), whole((pixels, channels))),
        out_shape=(
            jax.ShapeDtypeStruct((frames, pixels, channels), bf16),
            jax.ShapeDtypeStruct((pixels, channels), bf16),
        ),
        scratch_shapes=[
            pltpu.VMEM((frames * pixels, channels), f32),
            pltpu.VMEM((wide, channels), bf16),
        ],
        compiler_params=params(),
        cost_estimate=cost(15),
        name="conv_forward",
    )(views, spatial, shift)


def back_part(views_ref, w_ref, r):
    channels = w_ref.shape[0]
    x = rows_of(views_ref, 2 - r)
    x = jnp.concatenate(
        [x[:, (2 - s) * channels : (3 - s) * channels] for s in range(3)], axis=1
    )
    return matmul_nt(x, w_ref[...])


def conv_back_kernel(views_ref, w_ref, acc_ref):
    r = pl.program_id(0)
    part = back_part(views_ref, w_ref, r)

    @pl.when(r == 0)
    def _():
        acc_ref[...] = part

    @pl.when(r != 0)
    def _():
        acc_ref[...] += part


def conv_back_start(views, spatial):
    frames, high, breadth, wide = views.shape
    channels = wide // 3
    rows = frames * (high - 2) * breadth
    return pl.pallas_call(
        conv_back_kernel,
        grid=(2,),
        in_specs=[whole(views.shape), pl.BlockSpec((channels, wide), lambda i: (0, i))],
        out_specs=whole((rows, channels)),
        out_shape=jax.ShapeDtypeStruct((rows, channels), f32),
        compiler_params=params(),
        cost_estimate=cost(12),
        name="conv_back_start",
    )(views, spatial)


def conv_back_end_kernel(
    count, views_ref, w_ref, part_ref, x_ref, mean_ref, scale_ref, same_ref, out_ref, acc_ref
):
    acc_ref[...] = part_ref[...] + back_part(views_ref, w_ref, 2)
    back_through_norm(count, x_ref, mean_ref, scale_ref, same_ref, out_ref, acc_ref)


def back_through_norm(count, x_ref, mean_ref, scale_ref, same_ref, out_ref, acc_ref):
    frames, pixels, _ = x_ref.shape

    def parts(f):
        normal = (x_ref[f].astype(f32) - mean_ref[f]) * scale_ref[f]
        gate = 1.0 / (1.0 + jnp.exp(-normal))
        slope = gate * (1.0 + normal * (1.0 - gate))
        return normal, slope

    sums = []
    for f in range(frames):
        normal, slope = parts(f)
        grad = acc_ref[f * pixels : (f + 1) * pixels] * slope
        acc_ref[f * pixels : (f + 1) * pixels] = grad
        sums.append(jnp.sum(grad, axis=0, keepdims=True))
        sums.append(jnp.sum(grad * normal, axis=0, keepdims=True))
    means = group_mean(sums, same_ref, count)
    for f in range(frames):
        normal = (x_ref[f].astype(f32) - mean_ref[f]) * scale_ref[f]
        one, two = means[2 * f : 2 * f + 1], means[2 * f + 1 : 2 * f + 2]
        grad = acc_ref[f * pixels : (f + 1) * pixels]
        out_ref[f] = (grad - one - normal * two) * scale_ref[f]


def conv_back_end(views, spatial, part, frames, mean, scale, same):
    count, pixels, channels = frames.shape
    return pl.pallas_call(
        lambda *refs: conv_back_end_kernel(pixels * (channels // GROUPS), *refs),
        grid=(1,),
        in_specs=[
            whole(views.shape),
            pl.BlockSpec((channels, 3 * channels), lambda i: (0, 2)),
            whole(part.shape),
            whole(frames.shape),
            whole(mean.shape),
            whole(scale.shape),
            whole(same.shape),
        ],
        out_specs=whole(frames.shape),
        out_shape=jax.ShapeDtypeStruct(frames.shape, f32),
        scratch_shapes=[pltpu.VMEM((count * pixels, channels), f32)],
        compiler_params=params(),
        cost_estimate=cost(12),
        name="conv_back_end",
    )(views, spatial, part, frames, mean, scale, same)


def neighbours(x_size, step):
    count = 2 * x_size
    return [(i, i + step) for i in range(count) if 0 <= i + step < count]


def body(latents, cotangent, timesteps, spatial_weight, temporal_weight, time_weight):
    clip_frames = latents[0]
    frame_count, height, breadth, channels = clip_frames.shape
    pixels = height * breadth
    out_count = frame_count // 2
    dp = lax.axis_size("dp")
    x_size = lax.axis_size("x")
    share = channels // dp
    half = share // 2
    core = lax.axis_index("core")
    core_scalar = core[None].astype(jnp.int32)
    frames = clip_frames.reshape(frame_count, pixels, channels)

    cot = cotangent[0].reshape(out_count, pixels, channels)
    following = lax.ppermute(cot[0], ("x", "core"), neighbours(x_size, -1))

    spatial = jnp.concatenate([spatial_weight, time_weight], axis=1)
    spatial_mine = lax.dynamic_slice_in_dim(spatial, core * half, half, axis=0)
    spatial_full = lax.all_gather(spatial_mine, ("dp", "core"), axis=0, tiled=True)
    group = lax.broadcasted_iota(jnp.int32, (channels, channels), 0) // (channels // GROUPS)
    same = (group == group.T).astype(f32)
    held = {}

    def activate(token):
        held["views"], held["mean"], held["scale"] = normalize(
            after(frames, token), same, breadth
        )
        return held["mean"]

    def turn(token):
        held["turned"] = turned_columns(after(held["views"], token))
        return held["turned"]

    temporal_full = gather_temporal(temporal_weight, (activate, turn))
    views, mean, scale = held["views"], held["mean"], held["scale"]
    turned = held["turned"].reshape(9, channels, frame_count * pixels)

    embedded = embedding(timesteps[0], time_weight.shape[1])
    hidden_back, back_views, shift_sum = hidden_gradient(cot, following, temporal_full, breadth)
    flat_back = hidden_back.reshape(frame_count * pixels, channels)
    pairs = jnp.concatenate([shift_sum, embedded[None]], axis=1)
    pairs = jnp.pad(pairs, ((0, 0), (0, PAIR_WIDTH - pairs.shape[1])))
    pairs = lax.all_gather(pairs, ("dp", "x", "core"), axis=0, tiled=True)

    one = weight_grad(turned, flat_back, 0, dp, core_scalar)
    chain_a = Chain(*one)
    two = weight_grad(turned, flat_back, 4, dp, core_scalar)
    chain_a.land(two[1])
    chain_b = Chain(*two)
    out_a = chain_a.launch()

    time_full = spatial_full[:, 9 * channels :]
    time_shift = jnp.dot(time_full.astype(f32), embedded, precision=lax.Precision.HIGHEST)
    hidden, end = conv_forward(views, spatial_full, after(time_shift, out_a)[None])
    chain_a.land(hidden)
    chain_b.land(hidden)
    before = lax.ppermute(end, ("x", "core"), neighbours(x_size, 1))
    out_a = chain_a.launch()
    out_b = chain_b.launch(before)
    last = last_grad(turned, flat_back, after(hidden, out_a, out_b), before, cot, dp, core_scalar)
    chain_a.land(last[1])
    chain_b.land(last[1])
    chain_c = Chain(*last)
    out_a = chain_a.launch()
    out_b = chain_b.launch(out_a)
    out_c = chain_c.launch(out_b)

    part = conv_back_start(after(back_views, out_c), spatial_full)
    chain_a.land(part)
    chain_b.land(part)
    chain_c.land(part)
    out_a = chain_a.launch()
    out_b = chain_b.launch(out_a)
    out_c = chain_c.launch(out_b)
    input_grad = conv_back_end(
        after(back_views, out_c), spatial_full, part, frames, mean, scale, same
    )
    chain_a.land(input_grad)
    chain_b.land(input_grad)
    chain_c.land(input_grad)
    out_c = chain_c.launch()
    first = chain_a.finish()
    out_b = chain_b.launch(out_c)

    downsampled = temporal_forward(after(hidden, first, out_b), before, temporal_full)
    chain_b.land(downsampled)
    chain_c.land(downsampled)
    rows = join_x(first[None], downsampled)
    second = chain_b.finish()[None]
    out_c = chain_c.launch(second)
    rows = jnp.concatenate([rows, join_x(second)])
    last_rows = join_core(join_x(chain_c.finish()[None]))[0]
    rows = join_core(rows)
    downsampled = downsampled.reshape(1, out_count, height, breadth, channels)
    input_grad = input_grad.reshape(1, frame_count, height, breadth, channels)

    mine = lax.dynamic_slice_in_dim(
        pairs[:, :channels], lax.axis_index("dp") * share, share, axis=1
    )
    time_grad = lax.dot_general(
        mine,
        pairs[:, channels : channels + time_weight.shape[1]],
        (((0,), (0,)), ((), ())),
        precision=lax.Precision.HIGHEST,
        preferred_element_type=f32,
    )

    spatial_grad = jnp.concatenate(
        [rows[i, j] for i in range(2) for j in range(4)] + [last_rows[0]], axis=1
    )
    temporal_grad = jnp.concatenate([last_rows[1 + k] for k in range(3)], axis=1)
    return (downsampled, input_grad, spatial_grad, temporal_grad, time_grad)


def solution(mesh):
    dp, tm = mesh.devices.shape
    fine = Mesh(mesh.devices.reshape(dp, tm // 2, 2), ("dp", "x", "core"))
    placed = (
        P("dp", ("x", "core"), None, None, None),
        P("dp", ("x", "core"), None, None, None),
        P("dp"),
        P("dp", None),
        P("dp", None),
        P("dp", None),
    )
    return jax.shard_map(
        body,
        mesh=fine,
        in_specs=placed,
        out_specs=(
            P("dp", ("x", "core"), None, None, None),
            P("dp", ("x", "core"), None, None, None),
            P("dp", None),
            P("dp", None),
            P("dp", None),
        ),
        check_vma=False,
    )
```
